512 devices in a mesh: sess: 16 (over z_hi, x), ctx: 32 (over y, z_lo, core).
Axes of the slice: x: 4, y: 8, z: 8 (z_hi: 4, z_lo: 2; z = z_hi * 2 + z_lo), core: 2. Of those that a mesh axis runs over, the one named last changes fastest.
Arguments:
- query_rows: bfloat16 [16, 2048, 4096], P('sess', 'ctx'), may hold values from -6 to 6
- key_rows: bfloat16 [16, 2048, 4096], P('sess', 'ctx'), may hold values from -6 to 6
- value_rows: bfloat16 [16, 2048, 4096], P('sess', 'ctx'), may hold values from -6 to 6
- seg_starts: int32 [16, 4], P('sess'), may hold values from 0 to 2047, as said below
- norm_gain: float32 [4096], replicated, may hold values from 0.1 to 1.9
Outputs:
- attended: bfloat16 [16, 2048, 4096], P('sess', 'ctx')
The draws below stay inside these ranges and needn't reach their ends.
Inputs may be any that keep to these rules, and one draw needn't show every extreme that they name: `seg_starts`: within each session the starts rise strictly, the first is 0 and the last is 2047.
All inputs are finite; a program needn't handle non-finite values.
Results may differ from the reference program's by a relative error of at most 0.0049.
Values sent between devices are 32-bit elements; how exact they have to be, the bound alone decides.
A program may use at most 192 MiB of HBM per device.

```python
import jax
import jax.numpy as jnp
from jax import lax

HEADS = 32
HD = 128
TOK_DEV = 64
SEGS = 4
LENGTH = 2048
SESSIONS = 16


def draw_seg_starts(key, part):

    def one_row(row_key):
        inner = jax.random.permutation(row_key, LENGTH - 2)[:SEGS - 2] + 1
        picked = jnp.sort(inner.astype(jnp.int32))
        first = jnp.zeros((1,), jnp.int32)
        final = jnp.full((1,), LENGTH - 1, jnp.int32)
        return jnp.concatenate([first, picked, final]).astype(jnp.int32)
    row_keys = jax.random.split(jax.random.fold_in(key, 7), SESSIONS)
    return jax.vmap(one_row)(row_keys)


def block_levels(own_key, dims, cuts, low, largest):
    loudness, own = 1.0, jax.random.fold_in(own_key, 6)
    for position, parts in cuts:
        draws = jnp.exp(jax.random.uniform(jax.random.fold_in(own, position), (parts,), jnp.float32, low / len(cuts), largest / len(cuts)))
        loudness = loudness * jnp.repeat(draws, dims[position] // parts).reshape([-1 if axis == position else 1 for axis in range(len(dims))])
    return loudness


def noise(rng, extent, deviation, bound, cuts=(), kind=jnp.bfloat16):
    loudness = block_levels(rng, extent, cuts, -0.22, 0.18) if cuts else 1.0
    array = jax.random.normal(rng, extent, jnp.float32) * deviation * loudness
    return jnp.minimum(jnp.maximum(array, -bound), bound).astype(kind)


def setup_inputs(seed: int = 0) -> dict:
    arg_keys = jax.random.split(jax.random.key(seed), 6)
    return {
        "query_rows": noise(arg_keys[0], (SESSIONS, LENGTH, HEADS * HD), 1.0, 6.0, ((0, 16), (1, 32))),
        "key_rows": noise(arg_keys[1], (SESSIONS, LENGTH, HEADS * HD), 1.0, 6.0, ((0, 16), (1, 32))),
        "value_rows": noise(arg_keys[2], (SESSIONS, LENGTH, HEADS * HD), 1.0, 6.0, ((0, 16), (1, 32))),
        "seg_starts": draw_seg_starts(jax.random.fold_in(arg_keys[5], 71), 0),
        "norm_gain": jnp.clip(1.0 + 0.18 * jax.random.normal(arg_keys[4], (HEADS * HD,), jnp.float32), 0.1, 1.9),
    }


def one_session(packed):
    query_rows, key_rows, value_rows, start_list = packed
    blocks = LENGTH // TOK_DEV
    positions = jnp.arange(LENGTH, dtype=jnp.int32)
    seg_ids = lax.optimization_barrier(jnp.sum((start_list[None, :] <= positions[:, None]).astype(jnp.int32), axis=1))
    query_blocks = query_rows.reshape(blocks, TOK_DEV, HEADS, HD)
    key_blocks = key_rows.reshape(blocks, TOK_DEV, HEADS, HD)
    value_blocks = value_rows.reshape(blocks, TOK_DEV, HEADS, HD)
    seg_blocks = seg_ids.reshape(blocks, TOK_DEV)
    causal = jnp.arange(TOK_DEV)[:, None] >= jnp.arange(TOK_DEV)[None, :]

    def step(state, inputs):
        query_b, key_b, value_b, seg_b, index = inputs
        block_start = (index * TOK_DEV).astype(jnp.int32)
        prior_count = jnp.sum((start_list < block_start).astype(jnp.int32))
        query_f = query_b.astype(jnp.float32)
        key_f = key_b.astype(jnp.float32)
        value_f = value_b.astype(jnp.float32)
        scores = jnp.einsum('the,uhe->htu', query_f, key_f)
        allowed = causal & (seg_b[:, None] == seg_b[None, :])
        weights = jnp.where(allowed[None], scores, 0.0).astype(jnp.bfloat16)
        intra = jnp.einsum('htu,uhe->the', weights.astype(jnp.float32), value_f)
        carried = state.astype(jnp.bfloat16).astype(jnp.float32)
        inter = jnp.einsum('the,hef->thf', query_f, carried)
        use_mask = (seg_b == prior_count).astype(jnp.float32)
        mixed = (intra + use_mask[:, None, None] * inter).reshape(TOK_DEV, HEADS * HD)
        last_seg = seg_b[-1]
        keep_mask = (seg_b == last_seg).astype(jnp.float32)
        summary = jnp.einsum('uhe,uhf->hef', key_f * keep_mask[:, None, None], value_f)
        reset_flag = (last_seg != prior_count).astype(jnp.float32)
        new_state = (1.0 - reset_flag) * state + summary
        return (new_state, mixed)
    initial = jnp.zeros((HEADS, HD, HD), jnp.float32)
    indices = jnp.arange(blocks, dtype=jnp.int32)
    final_state, mixed_all = lax.scan(step, initial, (query_blocks, key_blocks, value_blocks, seg_blocks, indices))
    return mixed_all.reshape(LENGTH, HEADS * HD)

def reference(query_rows, key_rows, value_rows, seg_starts, norm_gain):
    mixed = lax.map(one_session, (query_rows, key_rows, value_rows, seg_starts))
    scale_inv = lax.rsqrt(lax.optimization_barrier(jnp.mean(mixed * mixed, axis=-1, keepdims=True)) + 1e-05)
    return (mixed * scale_inv * norm_gain).astype(jnp.bfloat16)
```

```python
import functools

import jax
import jax.numpy as jnp
from jax import lax
from jax.experimental import pallas as pl
from jax.experimental.pallas import tpu as pltpu
from jax.sharding import PartitionSpec as P

HEADS = 32
HD = 128
OWN = 8
SUB = 2
ROWS = HD // SUB
CHUNKS = OWN * SUB
RING = 8
MESH = pl.DeviceIdType.MESH
F32 = jnp.float32


def rows_at(i):
    return pl.ds(pl.multiple_of(i * ROWS, ROWS), ROWS)


def kernel(starts, q_ref, k_ref, v_ref, gain_ref, out_ref,
           own, kept, core_in, chip_far, chip_own, chip_in, scan_out, scan_in,
           back_out, back_in, core_out, carry_in, carry, mixed,
           sa, ra, sb, rb, sd, rd, se, re, sf, rf):
    me = lax.axis_index("ctx")
    core = me % 2
    half = (me // 2) % 2
    ring = me // 4
    tok = q_ref.shape[0]
    base = me * tok

    twin = {"ctx": me + 1 - 2 * core}
    across = {"ctx": me + 2 - 4 * half}
    ahead = {"ctx": (me + 4) % (4 * RING)}
    behind = {"ctx": (me + 4 * RING - 4) % (4 * RING)}

    barrier = pltpu.get_barrier_semaphore()
    for other in (twin, across, ahead, behind):
        pl.semaphore_signal(barrier, inc=1, device_id=other, device_id_type=MESH)

    start = [starts[0, n] for n in range(4)]

    def keep(low, size):
        inside = [jnp.where((s >= low) & (s < low + size), 1, 0) for s in start]
        return jnp.where(sum(inside) == 0, 1.0, 0.0).astype(F32)

    chip_base = (me // 2) * (2 * tok)
    ring_base = ring * (4 * tok)
    keep_core0 = keep(chip_base, tok)
    keep_core1 = keep(chip_base + tok, tok)
    keep_chip0 = keep(ring_base, 2 * tok)
    keep_chip1 = keep(ring_base + 2 * tok, 2 * tok)
    keep_ring = keep(ring_base, 4 * tok)
    one, nil = jnp.float32(1.0), jnp.float32(0.0)
    first_core, first_half = core == 0, half == 0
    a_own = jnp.where(first_core, keep_core1, one)
    a_in = jnp.where(first_core, one, keep_core1)
    b_own = jnp.where(first_half, keep_chip1, one)
    b_in = jnp.where(first_half, one, keep_chip1)
    e_own, e_scan = jnp.where(first_half, one, nil), jnp.where(first_half, keep_chip0, one)
    p_in, p_scan = jnp.where(first_half, nil, one), jnp.where(first_half, one, keep_chip0)
    f_own, f_pre = jnp.where(first_core, one, nil), jnp.where(first_core, keep_core0, one)
    g_in, g_pre = jnp.where(first_core, nil, one), jnp.where(first_core, one, keep_core0)

    def segment(pos):
        return sum((s <= pos).astype(jnp.int32) for s in start)

    row = lax.broadcasted_iota(jnp.int32, (tok, 1), 0) + base
    col = lax.broadcasted_iota(jnp.int32, (1, tok), 1) + base
    seg_row, seg_col = segment(row), segment(col)
    prior = sum(jnp.where(s < base, 1, 0) for s in start)
    last = sum(jnp.where(s < base + tok, 1, 0) for s in start)
    use = jnp.where(seg_row == prior, 1.0, 0.0).astype(F32)
    allowed = (row >= col) & (seg_row == seg_col)
    keep_rows = jnp.where(seg_row == last, 1.0, 0.0).astype(k_ref.dtype)

    def head_cols(h):
        return pl.ds(pl.multiple_of(h * HD, HD), HD)

    def group(c, z):
        return (2 * c + z) * OWN

    kept[...] = k_ref[...] * keep_rows

    def send_core(z, j):
        return pltpu.make_async_remote_copy(
            src_ref=own.at[group(1 - core, z) + j], dst_ref=core_in.at[z * OWN + j],
            send_sem=sa.at[z * OWN + j], recv_sem=ra.at[z * OWN + j],
            device_id=twin, device_id_type=MESH)

    def send_chip(i):
        return pltpu.make_async_remote_copy(
            src_ref=chip_far.at[rows_at(i)], dst_ref=chip_in.at[rows_at(i)],
            send_sem=sb.at[i], recv_sem=rb.at[i], device_id=across, device_id_type=MESH)

    def send_scan(i):
        return pltpu.make_async_remote_copy(
            src_ref=scan_out.at[rows_at(i)], dst_ref=scan_in.at[rows_at(i)],
            send_sem=sd.at[i], recv_sem=rd.at[i], device_id=ahead, device_id_type=MESH)

    def send_back(i):
        return pltpu.make_async_remote_copy(
            src_ref=back_out.at[rows_at(i)], dst_ref=back_in.at[rows_at(i)],
            send_sem=se.at[i], recv_sem=re.at[i], device_id=across, device_id_type=MESH)

    def send_carry(z, i):
        n = z * CHUNKS + i
        return pltpu.make_async_remote_copy(
            src_ref=core_out.at[rows_at(n)], dst_ref=carry_in.at[rows_at(n)],
            send_sem=sf.at[n], recv_sem=rf.at[n], device_id=twin, device_id_type=MESH)

    def summary(h):
        own[h] = lax.dot_general(
            kept[:, head_cols(h)], v_ref[:, head_cols(h)], (((0,), (0,)), ((), ())),
            preferred_element_type=F32)

    for j in range(OWN):
        summary(group(1 - core, 1 - half) + j)
    pl.semaphore_wait(barrier, 4)
    for j in range(OWN):
        send_core(1 - half, j).start()
    for j in range(OWN):
        summary(group(core, 1 - half) + j)
        summary(group(1 - core, half) + j)
        send_core(half, j).start()

    def far(j, _):
        n = (1 - half) * OWN + j
        send_core(1 - half, j).wait_recv()
        total = a_own * own[group(core, 1 - half) + j] + a_in * core_in[n]
        chip_far[pl.ds(pl.multiple_of(j * HD, HD), HD)] = total
        for s in range(SUB):
            send_chip(j * SUB + s).start()
        return 0

    lax.fori_loop(0, OWN, far, 0)
    for j in range(OWN):
        summary(group(core, half) + j)

    def near(j, _):
        n = half * OWN + j
        send_core(half, j).wait_recv()
        chip_own[pl.ds(pl.multiple_of(j * HD, HD), HD)] = (
            a_own * own[group(core, half) + j] + a_in * core_in[n])
        return 0

    lax.fori_loop(0, OWN, near, 0)

    @pl.when(ring == 0)
    def _():
        scan_in[...] = jnp.zeros_like(scan_in)

    def spread(z, i, prefix):
        h, sub = group(core, z) + i // SUB, pl.ds(pl.multiple_of((i % SUB) * ROWS, ROWS), ROWS)
        n = z * CHUNKS + i
        core_out[rows_at(n)] = f_own * own[h, sub] + f_pre * prefix
        send_carry(z, i).start()
        carry[rows_at(n)] = (g_in * core_in[z * OWN + i // SUB, sub] + g_pre * prefix).astype(carry.dtype)

    def intra(h):
        cols = head_cols(h)
        scores = lax.dot_general(
            q_ref[:, cols], k_ref[:, cols], (((1,), (1,)), ((), ())), preferred_element_type=F32)
        weights = jnp.where(allowed, scores, 0.0).astype(v_ref.dtype)
        mixed[:, cols] = jnp.dot(weights, v_ref[:, cols], preferred_element_type=F32)

    def scan(i, _):
        send_chip(i).wait_recv()
        arrived, mine = chip_in[rows_at(i)], chip_own[rows_at(i)]

        @pl.when(ring > 0)
        def _():
            send_scan(i).wait_recv()

        prefix = scan_in[rows_at(i)]

        @pl.when(ring < RING - 1)
        def _():
            scan_out[rows_at(i)] = b_own * mine + b_in * arrived + keep_ring * prefix
            send_scan(i).start()

        back_out[rows_at(i)] = e_own * mine + e_scan * prefix
        send_back(i).start()
        spread(half, i, p_in * arrived + p_scan * prefix)
        for n in range(HEADS // CHUNKS):
            intra(i * (HEADS // CHUNKS) + n)
        return 0

    lax.fori_loop(0, CHUNKS, scan, 0)

    def back(i, _):
        send_back(i).wait_recv()
        spread(1 - half, i, back_in[rows_at(i)])
        return 0

    lax.fori_loop(0, CHUNKS, back, 0)

    def join(h, state, squares):
        cols = head_cols(h)
        inter = jnp.dot(q_ref[:, cols], state, preferred_element_type=F32)
        value = mixed[:, cols] + use * inter
        mixed[:, cols] = value
        return squares + value * value

    def join_own(n, squares):
        return join(group(core, 0) + n, carry[pl.ds(pl.multiple_of(n * HD, HD), HD)], squares)

    def join_in(n, squares):
        for s in range(SUB):
            send_carry(n // OWN, (n % OWN) * SUB + s).wait_recv()
        state = carry_in[pl.ds(pl.multiple_of(n * HD, HD), HD)].astype(carry.dtype)
        return join(group(1 - core, 0) + n, state, squares)

    squares = lax.fori_loop(0, 2 * OWN, join_own, jnp.zeros((tok, HD), F32))
    squares = lax.fori_loop(0, 2 * OWN, join_in, squares)
    mean = jnp.sum(squares, axis=-1, keepdims=True) * (1.0 / (HEADS * HD))
    scale = lax.rsqrt(mean + 1e-05)
    for h in range(HEADS):
        cols = slice(h * HD, (h + 1) * HD)
        out_ref[:, cols] = (mixed[:, cols] * scale * gain_ref[:, cols]).astype(out_ref.dtype)

    def drain(i, _):
        send_chip(i).wait_send()
        send_back(i).wait_send()
        send_carry(0, i).wait_send()
        send_carry(1, i).wait_send()

        @pl.when(ring < RING - 1)
        def _():
            send_scan(i).wait_send()

        return 0

    def drain_core(j, _):
        send_core(0, j).wait_send()
        send_core(1, j).wait_send()
        return 0

    lax.fori_loop(0, OWN, drain_core, 0)
    lax.fori_loop(0, CHUNKS, drain, 0)


def shards(query_rows, key_rows, value_rows, seg_starts, norm_gain):
    _, tok, width = query_rows.shape
    dma = pltpu.SemaphoreType.DMA
    vmem = pl.BlockSpec(memory_space=pltpu.VMEM)
    out = pl.pallas_call(
        kernel,
        out_shape=jax.ShapeDtypeStruct((tok, width), query_rows.dtype),
        in_specs=[pl.BlockSpec(memory_space=pltpu.SMEM), vmem, vmem, vmem, vmem],
        out_specs=vmem,
        scratch_shapes=[
            pltpu.VMEM((HEADS, HD, HD), F32),
            pltpu.VMEM((tok, width), key_rows.dtype),
            pltpu.VMEM((2 * OWN, HD, HD), F32),
            pltpu.VMEM((OWN * HD, HD), F32),
            pltpu.VMEM((OWN * HD, HD), F32),
            pltpu.VMEM((OWN * HD, HD), F32),
            pltpu.VMEM((OWN * HD, HD), F32),
            pltpu.VMEM((OWN * HD, HD), F32),
            pltpu.VMEM((OWN * HD, HD), F32),
            pltpu.VMEM((OWN * HD, HD), F32),
            pltpu.VMEM((2 * OWN * HD, HD), F32),
            pltpu.VMEM((2 * OWN * HD, HD), F32),
            pltpu.VMEM((2 * OWN * HD, HD), jnp.bfloat16),
            pltpu.VMEM((tok, width), F32),
            dma((2 * OWN,)), dma((2 * OWN,)),
            dma((CHUNKS,)), dma((CHUNKS,)),
            dma((CHUNKS,)), dma((CHUNKS,)),
            dma((CHUNKS,)), dma((CHUNKS,)),
            dma((2 * CHUNKS,)), dma((2 * CHUNKS,)),
        ],
        compiler_params=pltpu.CompilerParams(collective_id=0, has_side_effects=True),
    )(seg_starts, query_rows[0], key_rows[0], value_rows[0], norm_gain.reshape(1, width))
    return out.reshape(1, tok, width)


def solution(mesh):
    placed = (
        P("sess", "ctx", None),
        P("sess", "ctx", None),
        P("sess", "ctx", None),
        P("sess", None),
        P(),
    )
    return jax.shard_map(
        shards, mesh=mesh, in_specs=placed, out_specs=P("sess", "ctx", None), check_vma=False
    )
```

```python
import jax
import jax.numpy as jnp
from jax import lax
from jax.experimental import pallas as pl
from jax.experimental.pallas import tpu as pltpu
from jax.sharding import PartitionSpec as P

HEADS = 32
HD = 128
OWN = 8
SUB = 4
ROWS = HD // SUB
CHUNKS = OWN * SUB
RING = 8
MID = RING // 2
HOP = 8
BACK = 9
DRAINED = 38
MESH = pl.DeviceIdType.MESH
F32 = jnp.float32


def rows_at(i):
    return pl.ds(pl.multiple_of(i * ROWS, ROWS), ROWS)


def head_rows(n):
    return pl.ds(pl.multiple_of(n * HD, HD), HD)


def head_cols(h):
    return pl.ds(pl.multiple_of(h * HD, HD), HD)


def kernel(starts_hbm, q_hbm, k_hbm, v_hbm, gain_hbm, out_ref,
           starts, q_ref, k_ref, v_ref, gain_ref,
           own, kept, core_in, chip_far, chip_own, chip_in, total,
           fore_out, fore_in, local_out, local_in, rear_out, rear_in,
           back_out, back_in, core_out, carry_in, carry, mixed,
           loads, core_sent, core_got, chip_sent, chip_got, fore_sent, fore_got,
           local_sent, local_got, rear_sent, rear_got, back_sent, back_got, carry_sent, carry_got):
    me = lax.axis_index("ctx")
    core = me % 2
    half = (me // 2) % 2
    ring = me // 4
    tok = q_ref.shape[0]
    base = me * tok

    twin = {"ctx": me + 1 - 2 * core}
    across = {"ctx": me + 2 - 4 * half}
    ahead = {"ctx": (me + 4) % (4 * RING)}
    behind = {"ctx": (me + 4 * RING - 4) % (4 * RING)}

    barrier = pltpu.get_barrier_semaphore()
    for other in (twin, across, ahead, behind):
        pl.semaphore_signal(barrier, inc=1, device_id=other, device_id_type=MESH)

    fetches = [
        pltpu.make_async_copy(src, dst, loads.at[n])
        for n, (src, dst) in enumerate((
            (starts_hbm, starts), (k_hbm, k_ref), (v_hbm, v_ref), (q_hbm, q_ref), (gain_hbm, gain_ref)))]
    for fetch in fetches:
        fetch.start()
    fetches[0].wait()

    start = [starts[0, n] for n in range(4)]

    def keep(low, size):
        inside = [jnp.where((s >= low) & (s < low + size), 1, 0) for s in start]
        return jnp.where(sum(inside) == 0, 1.0, 0.0).astype(F32)

    chip_base = (me // 2) * (2 * tok)
    span = 4 * tok
    ring_base = ring * span
    keep_core0 = keep(chip_base, tok)
    keep_core1 = keep(chip_base + tok, tok)
    keep_chip0 = keep(ring_base, 2 * tok)
    keep_chip1 = keep(ring_base + 2 * tok, 2 * tok)
    keep_ring = keep(ring_base, span)
    keep_local = keep(MID * span, ring_base - MID * span)
    one, nil = jnp.float32(1.0), jnp.float32(0.0)
    keep_rear = jnp.where(ring >= MID, nil, keep(ring_base + span, (MID - 1 - ring) * span))
    first_core, first_half = core == 0, half == 0
    a_own = jnp.where(first_core, keep_core1, one)
    a_in = jnp.where(first_core, one, keep_core1)
    b_own = jnp.where(first_half, keep_chip1, one)
    b_in = jnp.where(first_half, one, keep_chip1)
    e_own, e_scan = jnp.where(first_half, one, nil), jnp.where(first_half, keep_chip0, one)
    p_in, p_scan = jnp.where(first_half, nil, one), jnp.where(first_half, one, keep_chip0)
    f_own, f_pre = jnp.where(first_core, one, nil), jnp.where(first_core, keep_core0, one)
    g_in, g_pre = jnp.where(first_core, nil, one), jnp.where(first_core, one, keep_core0)

    def segment(pos):
        return sum((s <= pos).astype(jnp.int32) for s in start)

    row = lax.broadcasted_iota(jnp.int32, (tok, 1), 0) + base
    col = lax.broadcasted_iota(jnp.int32, (1, tok), 1) + base
    seg_row, seg_col = segment(row), segment(col)
    prior = sum(jnp.where(s < base, 1, 0) for s in start)
    last = sum(jnp.where(s < base + tok, 1, 0) for s in start)
    use = jnp.where(seg_row == prior, 1.0, 0.0).astype(F32)
    allowed = (row >= col) & (seg_row == seg_col)
    keep_rows = jnp.where(seg_row == last, 1.0, 0.0).astype(k_ref.dtype)

    def group(c, z):
        return (2 * c + z) * OWN

    def remote(src, dst, sent, got, device):
        return pltpu.make_async_remote_copy(
            src_ref=src, dst_ref=dst, send_sem=sent, recv_sem=got,
            device_id=device, device_id_type=MESH)

    def send_core(z, j):
        return remote(own.at[head_rows(group(1 - core, z) + j)], core_in.at[head_rows(z * OWN + j)],
                      core_sent, core_got.at[z * OWN + j], twin)

    def send_chip(i):
        return remote(chip_far.at[rows_at(i)], chip_in.at[rows_at(i)],
                      chip_sent, chip_got.at[i], across)

    def send_fore(i):
        return remote(fore_out.at[rows_at(i)], fore_in.at[rows_at(i)],
                      fore_sent, fore_got.at[i], ahead)

    def send_local(i):
        return remote(local_out.at[rows_at(i)], local_in.at[rows_at(i)],
                      local_sent, local_got.at[i], ahead)

    def send_rear(i):
        return remote(rear_out.at[rows_at(i)], rear_in.at[rows_at(i)],
                      rear_sent, rear_got.at[i], behind)

    def send_back(i):
        return remote(back_out.at[rows_at(i)], back_in.at[rows_at(i)],
                      back_sent, back_got.at[i], across)

    def send_carry(n):
        return remote(core_out.at[rows_at(n)], carry_in.at[rows_at(n)],
                      carry_sent, carry_got.at[n], twin)

    def summaries(first):
        states = [lax.dot_general(
            kept[:, head_cols(first + j)], v_ref[:, head_cols(first + j)],
            (((0,), (0,)), ((), ())), preferred_element_type=F32) for j in range(OWN)]
        for j in range(OWN):
            own[head_rows(first + j)] = states[j]

    fetches[1].wait()
    kept[...] = k_ref[...] * keep_rows
    fetches[2].wait()
    summaries(group(1 - core, 1 - half))
    summaries(group(core, 1 - half))
    pl.semaphore_wait(barrier, 4)
    for j in range(OWN):
        send_core(1 - half, j).start()
    summaries(group(1 - core, half))
    for j in range(OWN):
        send_core(half, j).start()
    summaries(group(core, half))

    def chip_total(z, j):
        send_core(z, j).wait_recv()
        return a_own * own[head_rows(group(core, z) + j)] + a_in * core_in[head_rows(z * OWN + j)]

    def far(j, _):
        chip_far[head_rows(j)] = chip_total(1 - half, j)
        for s in range(SUB):
            send_chip(j * SUB + s).start()
        return 0

    def near(j, _):
        chip_own[head_rows(j)] = chip_total(half, j)
        return 0

    lax.fori_loop(0, OWN, far, 0)
    lax.fori_loop(0, OWN, near, 0)

    @pl.when(ring == 0)
    def _():
        fore_in[...] = jnp.zeros_like(fore_in)

    @pl.when(ring == MID)
    def _():
        local_in[...] = jnp.zeros_like(local_in)

    @pl.when(ring == MID - 1)
    def _():
        rear_in[...] = jnp.zeros_like(rear_in)

    def intra(n, _):
        cols = [head_cols(n * 8 + m) for m in range(8)]
        scores = [lax.dot_general(
            q_ref[:, c], k_ref[:, c], (((1,), (1,)), ((), ())), preferred_element_type=F32)
            for c in cols]
        weights = [jnp.where(allowed, s, 0.0).astype(v_ref.dtype) for s in scores]
        values = [jnp.dot(w, v_ref[:, c], preferred_element_type=F32) for w, c in zip(weights, cols)]
        for c, value in zip(cols, values):
            mixed[:, c] = value
        return 0

    fetches[3].wait()
    fetches[4].wait()
    early = ring >= MID

    @pl.when(early)
    def _():
        lax.fori_loop(0, HEADS // 8, intra, 0)

    def spread(z, i, prefix):
        n = z * CHUNKS + i
        core_out[rows_at(n)] = f_own * own[rows_at(group(core, z) * SUB + i)] + f_pre * prefix
        send_carry(n).start()
        carry[rows_at(n)] = (g_in * core_in[rows_at(n)] + g_pre * prefix).astype(carry.dtype)

    def finish(i, prefix):
        arrived, mine = chip_in[rows_at(i)], chip_own[rows_at(i)]
        back_out[rows_at(i)] = e_own * mine + e_scan * prefix
        send_back(i).start()
        spread(half, i, p_in * arrived + p_scan * prefix)

    last_fore = MID + 1
    lag_local = HOP * (ring - MID)
    lag_fore = HOP * ring
    lag_rear = HOP * ((RING + MID - 1 - ring) % RING)
    lag_back = jnp.maximum(jnp.where(ring <= last_fore, lag_fore, lag_rear) + BACK, DRAINED)

    def active(s, lag):
        return (s >= lag) & (s < lag + CHUNKS)

    def step(s, _):
        @pl.when(s < CHUNKS)
        def _():
            send_chip(s).wait_recv()
            total[rows_at(s)] = b_own * chip_own[rows_at(s)] + b_in * chip_in[rows_at(s)]

        @pl.when((ring >= MID) & active(s, lag_local))
        def _():
            i = s - lag_local

            @pl.when(ring > MID)
            def _():
                send_local(i).wait_recv()

            @pl.when(ring < RING - 1)
            def _():
                local_out[rows_at(i)] = total[rows_at(i)] + keep_ring * local_in[rows_at(i)]
                send_local(i).start()

        @pl.when((ring <= last_fore) & active(s, lag_fore))
        def _():
            i = s - lag_fore

            @pl.when(ring > 0)
            def _():
                send_fore(i).wait_recv()

            prefix = fore_in[rows_at(i)]

            @pl.when(ring < last_fore)
            def _():
                fore_out[rows_at(i)] = total[rows_at(i)] + keep_ring * prefix
                send_fore(i).start()

            finish(i, prefix)

        @pl.when(((ring < MID) | (ring > last_fore)) & active(s, lag_rear))
        def _():
            i = s - lag_rear

            @pl.when(ring != MID - 1)
            def _():
                send_rear(i).wait_recv()

            @pl.when((ring < MID) | (ring == RING - 1))
            def _():
                rear_out[rows_at(i)] = rear_in[rows_at(i)] + keep_rear * total[rows_at(i)]
                send_rear(i).start()

            @pl.when(ring > last_fore)
            def _():
                finish(i, local_in[rows_at(i)] + keep_local * rear_in[rows_at(i)])

        @pl.when(active(s, lag_back))
        def _():
            i = s - lag_back
            send_back(i).wait_recv()
            spread(1 - half, i, back_in[rows_at(i)])

        return 0

    lax.fori_loop(0, lag_back + CHUNKS, step, 0)

    @pl.when(jnp.logical_not(early))
    def _():
        lax.fori_loop(0, HEADS // 8, intra, 0)

    def settle(j, squares):
        heads, states = [], []
        for z in (half, 1 - half):
            heads.append(group(core, z) + j)
            states.append(carry[head_rows(z * OWN + j)])
        for z in (half, 1 - half):
            for s in range(SUB):
                send_carry(z * CHUNKS + j * SUB + s).wait_recv()
            heads.append(group(1 - core, z) + j)
            states.append(carry_in[head_rows(z * OWN + j)].astype(carry.dtype))
        cols = [head_cols(h) for h in heads]
        inter = [jnp.dot(q_ref[:, c], state, preferred_element_type=F32) for c, state in zip(cols, states)]
        values = [mixed[:, c] + use * part for c, part in zip(cols, inter)]
        for c, value in zip(cols, values):
            mixed[:, c] = value
        return squares + sum(value * value for value in values)

    squares = lax.fori_loop(0, OWN, settle, jnp.zeros((tok, HD), F32))
    mean = jnp.sum(squares, axis=-1, keepdims=True) * (1.0 / (HEADS * HD))
    scale = lax.rsqrt(mean + 1e-05)
    for h in range(HEADS):
        cols = slice(h * HD, (h + 1) * HD)
        out_ref[:, cols] = (mixed[:, cols] * scale * gain_ref[:, cols]).astype(out_ref.dtype)

    for z in range(2):
        part = pl.ds(pl.multiple_of(group(1 - core, z) * HD, HD), OWN * HD)
        remote(own.at[part], core_in.at[pl.ds(z * OWN * HD, OWN * HD)], core_sent, core_got.at[0], twin).wait_send()
    remote(chip_far, chip_in, chip_sent, chip_got.at[0], across).wait_send()
    remote(back_out, back_in, back_sent, back_got.at[0], across).wait_send()
    remote(core_out, carry_in, carry_sent, carry_got.at[0], twin).wait_send()

    @pl.when(ring < last_fore)
    def _():
        remote(fore_out, fore_in, fore_sent, fore_got.at[0], ahead).wait_send()

    @pl.when((ring >= MID) & (ring < RING - 1))
    def _():
        remote(local_out, local_in, local_sent, local_got.at[0], ahead).wait_send()

    @pl.when((ring < MID) | (ring == RING - 1))
    def _():
        remote(rear_out, rear_in, rear_sent, rear_got.at[0], behind).wait_send()


def shards(query_rows, key_rows, value_rows, seg_starts, norm_gain):
    _, tok, width = query_rows.shape
    dma = pltpu.SemaphoreType.DMA
    hbm = pl.BlockSpec(memory_space=pltpu.HBM)
    block = pltpu.VMEM((tok, width), key_rows.dtype)
    states = lambda heads: pltpu.VMEM((heads * HD, HD), F32)
    one = dma(())
    stay = lambda x: pltpu.with_memory_space_constraint(x, pltpu.HBM)
    out = pl.pallas_call(
        kernel,
        out_shape=jax.ShapeDtypeStruct((tok, width), query_rows.dtype),
        in_specs=[hbm] * 5,
        out_specs=pl.BlockSpec(memory_space=pltpu.VMEM),
        scratch_shapes=[
            pltpu.SMEM((1, 4), jnp.int32), block, block, block, pltpu.VMEM((1, width), F32),
            states(HEADS), block, states(2 * OWN),
            states(OWN), states(OWN), states(OWN), states(OWN),
            states(OWN), states(OWN), states(OWN), states(OWN), states(OWN), states(OWN),
            states(OWN), states(OWN), states(2 * OWN), states(2 * OWN),
            pltpu.VMEM((2 * OWN * HD, HD), jnp.bfloat16),
            pltpu.VMEM((tok, width), F32),
            dma((5,)),
            one, dma((2 * OWN,)), one, dma((CHUNKS,)), one, dma((CHUNKS,)),
            one, dma((CHUNKS,)), one, dma((CHUNKS,)), one, dma((CHUNKS,)), one, dma((2 * CHUNKS,)),
        ],
        compiler_params=pltpu.CompilerParams(
            collective_id=0, has_side_effects=True, vmem_limit_bytes=32 * 1024 * 1024),
    )(stay(seg_starts), stay(query_rows[0]), stay(key_rows[0]), stay(value_rows[0]),
      stay(norm_gain.reshape(1, width)))
    return out.reshape(1, tok, width)


def solution(mesh):
    placed = (
        P("sess", "ctx", None),
        P("sess", "ctx", None),
        P("sess", "ctx", None),
        P("sess", None),
        P(),
    )
    return jax.shard_map(
        shards, mesh=mesh, in_specs=placed, out_specs=P("sess", "ctx", None), check_vma=False
    )
```

```python
import jax
import jax.numpy as jnp
from jax import lax
from jax.experimental import pallas as pl
from jax.experimental.pallas import tpu as pltpu
from jax.sharding import PartitionSpec as P

HEADS = 32
HD = 128
OWN = 8
SUB = 4
ROWS = HD // SUB
CHUNKS = OWN * SUB
RING = 8
MID = RING // 2
HOP = 8
BACK = 9
JOIN = 8
DRAINED = 44
MESH = pl.DeviceIdType.MESH
F32 = jnp.float32


def rows_at(i):
    return pl.ds(pl.multiple_of(i * ROWS, ROWS), ROWS)


def head_rows(n):
    return pl.ds(pl.multiple_of(n * HD, HD), HD)


def head_cols(h):
    return pl.ds(pl.multiple_of(h * HD, HD), HD)


def kernel(starts_hbm, q_hbm, k_hbm, v_hbm, gain_hbm, out_ref,
           starts, q_ref, k_ref, v_ref, gain_ref,
           own, core_in, chip_far, chip_own, chip_in, total,
           fore_out, fore_in, local_out, local_in, rear_out, rear_in,
           back_out, back_in, core_out, carry_in, carry, mixed, squares,
           loads, core_sent, core_got, chip_sent, chip_got, fore_sent, ring_got,
           local_sent, rear_sent, back_sent, back_got, carry_sent, carry_got):
    me = lax.axis_index("ctx")
    core = me % 2
    half = (me // 2) % 2
    ring = me // 4
    tok = q_ref.shape[0]
    base = me * tok

    twin = {"ctx": me + 1 - 2 * core}
    across = {"ctx": me + 2 - 4 * half}
    ahead = {"ctx": (me + 4) % (4 * RING)}
    behind = {"ctx": (me + 4 * RING - 4) % (4 * RING)}

    last_fore = MID + 1

    def group(c, z):
        return (2 * c + z) * OWN

    def group_rows(c, z):
        return pl.ds(pl.multiple_of(group(c, z) * HD, HD), OWN * HD)

    order = [(1 - core, 1 - half), (core, 1 - half), (1 - core, half), (core, half)]
    fetch_starts = pltpu.make_async_copy(starts_hbm, starts, loads.at[0])
    fetch_keys = [pltpu.make_async_copy(
        k_hbm.at[:, group_rows(*g)], k_ref.at[:, group_rows(*g)], loads.at[1 + n]) for n, g in enumerate(order)]
    fetch_values = [pltpu.make_async_copy(
        v_hbm.at[:, group_rows(*g)], v_ref.at[:, group_rows(*g)], loads.at[5 + n]) for n, g in enumerate(order)]
    fetch_rest = [pltpu.make_async_copy(q_hbm, q_ref, loads.at[9]),
                  pltpu.make_async_copy(gain_hbm, gain_ref, loads.at[10])]
    fetch_starts.start()
    fetch_keys[0].start()
    fetch_values[0].start()
    barrier = pltpu.get_barrier_semaphore()
    for other in (twin, across, ahead, behind):
        pl.semaphore_signal(barrier, inc=1, device_id=other, device_id_type=MESH)

    for n in range(1, 4):
        fetch_keys[n].start()
        fetch_values[n].start()
    for fetch in fetch_rest:
        fetch.start()
    fetch_starts.wait()

    start = [starts[0, n] for n in range(4)]

    def keep(low, size):
        inside = [jnp.where((s >= low) & (s < low + size), 1, 0) for s in start]
        return jnp.where(sum(inside) == 0, 1.0, 0.0).astype(F32)

    chip_base = (me // 2) * (2 * tok)
    span = 4 * tok
    ring_base = ring * span
    keep_core0 = keep(chip_base, tok)
    keep_core1 = keep(chip_base + tok, tok)
    keep_chip0 = keep(ring_base, 2 * tok)
    keep_chip1 = keep(ring_base + 2 * tok, 2 * tok)
    keep_ring = keep(ring_base, span)
    keep_local = keep(MID * span, ring_base - MID * span)
    one, nil = jnp.float32(1.0), jnp.float32(0.0)
    keep_rear = jnp.where(ring >= MID, nil, keep(ring_base + span, (MID - 1 - ring) * span))
    first_core, first_half = core == 0, half == 0
    a_own = jnp.where(first_core, keep_core1, one)
    a_in = jnp.where(first_core, one, keep_core1)
    b_own = jnp.where(first_half, keep_chip1, one)
    b_in = jnp.where(first_half, one, keep_chip1)
    e_own, e_scan = jnp.where(first_half, one, nil), jnp.where(first_half, keep_chip0, one)
    p_in, p_scan = jnp.where(first_half, nil, one), jnp.where(first_half, one, keep_chip0)
    f_own, f_pre = jnp.where(first_core, one, nil), jnp.where(first_core, keep_core0, one)
    g_in, g_pre = jnp.where(first_core, nil, one), jnp.where(first_core, one, keep_core0)

    def segment(pos):
        return sum((s <= pos).astype(jnp.int32) for s in start)

    row = lax.broadcasted_iota(jnp.int32, (tok, 1), 0) + base
    col = lax.broadcasted_iota(jnp.int32, (1, tok), 1) + base
    seg_row, seg_col = segment(row), segment(col)
    prior = sum(jnp.where(s < base, 1, 0) for s in start)
    last = sum(jnp.where(s < base + tok, 1, 0) for s in start)
    use = jnp.where(seg_row == prior, 1.0, 0.0).astype(F32)
    allowed = (row >= col) & (seg_row == seg_col)
    keep_rows = jnp.where(seg_row == last, 1.0, 0.0).astype(k_ref.dtype)

    def remote(src, dst, sent, got, device):
        return pltpu.make_async_remote_copy(
            src_ref=src, dst_ref=dst, send_sem=sent, recv_sem=got,
            device_id=device, device_id_type=MESH)

    def send_core(j):
        z = 1 - half
        return remote(own.at[head_rows(group(1 - core, z) + j)], core_in.at[head_rows(z * OWN + j)],
                      core_sent, core_got.at[j], twin)

    def send_rest():
        return remote(own.at[group_rows(1 - core, half)], core_in.at[pl.ds(half * OWN * HD, OWN * HD)],
                      core_sent, core_got.at[OWN], twin)

    def send_chip(i):
        return remote(chip_far.at[rows_at(i)], chip_in.at[rows_at(i)],
                      chip_sent, chip_got.at[i], across)

    def send_fore(i):
        return remote(fore_out.at[rows_at(i)], fore_in.at[rows_at(i)],
                      fore_sent, ring_got.at[i], ahead)

    def local_lane(place):
        return jnp.where(place == last_fore, CHUNKS, 0)

    def send_local(i, place):
        return remote(local_out.at[rows_at(i)], local_in.at[rows_at(i)],
                      local_sent, ring_got.at[local_lane(place) + i], ahead)

    def send_rear(i):
        return remote(rear_out.at[rows_at(i)], rear_in.at[rows_at(i)],
                      rear_sent, ring_got.at[CHUNKS + i], behind)

    def send_back(i):
        return remote(back_out.at[rows_at(i)], back_in.at[rows_at(i)],
                      back_sent, back_got.at[i], across)

    def send_carry(n):
        return remote(core_out.at[head_rows(n)], carry_in.at[head_rows(n)],
                      carry_sent, carry_got.at[n], twin)

    def summaries(n):
        fetch_keys[n].wait()
        fetch_values[n].wait()
        first = group(*order[n])
        states = []
        for j in range(OWN):
            cols = head_cols(first + j)
            states.append(lax.dot_general(
                k_ref[:, cols] * keep_rows, v_ref[:, cols],
                (((0,), (0,)), ((), ())), preferred_element_type=F32))
        for j in range(OWN):
            own[head_rows(first + j)] = states[j]

    summaries(0)
    pl.semaphore_wait(barrier, 4)
    for j in range(OWN):
        send_core(j).start()
    summaries(1)

    def chip_total(z, j):
        return a_own * own[head_rows(group(core, z) + j)] + a_in * core_in[head_rows(z * OWN + j)]

    def far(j, _):
        send_core(j).wait_recv()
        chip_far[head_rows(j)] = chip_total(1 - half, j)
        for s in range(SUB):
            send_chip(j * SUB + s).start()
        return 0

    def near(j, _):
        chip_own[head_rows(j)] = chip_total(half, j)
        return 0

    lax.fori_loop(0, OWN, far, 0)
    summaries(2)
    send_rest().start()
    summaries(3)

    @pl.when(ring == 0)
    def _():
        fore_in[...] = jnp.zeros_like(fore_in)

    @pl.when(ring == MID)
    def _():
        local_in[...] = jnp.zeros_like(local_in)

    @pl.when(ring == MID - 1)
    def _():
        rear_in[...] = jnp.zeros_like(rear_in)

    def intra(n, _):
        cols = [head_cols(n * 8 + m) for m in range(8)]
        scores = [lax.dot_general(
            q_ref[:, c], k_ref[:, c], (((1,), (1,)), ((), ())), preferred_element_type=F32)
            for c in cols]
        weights = [jnp.where(allowed, s, 0.0).astype(v_ref.dtype) for s in scores]
        values = [jnp.dot(w, v_ref[:, c], preferred_element_type=F32) for w, c in zip(weights, cols)]
        for c, value in zip(cols, values):
            mixed[:, c] = value
        return 0

    for fetch in fetch_rest:
        fetch.wait()
    squares[...] = jnp.zeros_like(squares)
    lax.fori_loop(0, HEADS // 8, intra, 0)
    send_rest().wait_recv()
    lax.fori_loop(0, OWN, near, 0)

    def spread(z, i, prefix):
        n = z * CHUNKS + i
        core_out[rows_at(n)] = f_own * own[rows_at(group(core, z) * SUB + i)] + f_pre * prefix
        carry[rows_at(n)] = (g_in * core_in[rows_at(n)] + g_pre * prefix).astype(carry.dtype)

        @pl.when(i % SUB == SUB - 1)
        def _():
            send_carry(z * OWN + i // SUB).start()

    def finish(i, prefix):
        arrived, mine = chip_in[rows_at(i)], chip_own[rows_at(i)]
        back_out[rows_at(i)] = e_own * mine + e_scan * prefix
        send_back(i).start()
        spread(half, i, p_in * arrived + p_scan * prefix)

    lag_local = HOP * (ring - MID)
    lag_fore = HOP * ring
    lag_rear = HOP * ((RING + MID - 1 - ring) % RING)
    ends = (ring > MID) & (ring < RING - 1)
    lag_prefix = jnp.where(ring <= last_fore, lag_fore, lag_rear)
    lag_back = jnp.where(ends, lag_prefix + BACK, jnp.maximum(lag_prefix + 2 * BACK, DRAINED))
    lag_join = lag_back + SUB + JOIN

    def settle(j):
        heads, states = [], []
        for z in (half, 1 - half):
            heads.append(group(core, z) + j)
            states.append(carry[head_rows(z * OWN + j)])
        for z in (half, 1 - half):
            send_carry(z * OWN + j).wait_recv()
            heads.append(group(1 - core, z) + j)
            states.append(carry_in[head_rows(z * OWN + j)].astype(carry.dtype))
        cols = [head_cols(h) for h in heads]
        inter = [jnp.dot(q_ref[:, c], state, preferred_element_type=F32) for c, state in zip(cols, states)]
        values = [mixed[:, c] + use * part for c, part in zip(cols, inter)]
        for c, value in zip(cols, values):
            mixed[:, c] = value
        squares[...] += sum(value * value for value in values)

    def active(s, lag):
        return (s >= lag) & (s < lag + CHUNKS)

    def step(s, _):
        @pl.when(s < CHUNKS)
        def _():
            send_chip(s).wait_recv()
            total[rows_at(s)] = b_own * chip_own[rows_at(s)] + b_in * chip_in[rows_at(s)]

        @pl.when((ring >= MID) & active(s, lag_local))
        def _():
            i = s - lag_local

            @pl.when(ring > MID)
            def _():
                send_local(i, ring).wait_recv()

            @pl.when(ring < RING - 1)
            def _():
                local_out[rows_at(i)] = total[rows_at(i)] + keep_ring * local_in[rows_at(i)]
                send_local(i, ring + 1).start()

        @pl.when((ring <= last_fore) & active(s, lag_fore))
        def _():
            i = s - lag_fore

            @pl.when(ring > 0)
            def _():
                send_fore(i).wait_recv()

            prefix = fore_in[rows_at(i)]

            @pl.when(ring < last_fore)
            def _():
                fore_out[rows_at(i)] = total[rows_at(i)] + keep_ring * prefix
                send_fore(i).start()

            finish(i, prefix)

        @pl.when(((ring < MID) | (ring > last_fore)) & active(s, lag_rear))
        def _():
            i = s - lag_rear

            @pl.when(ring != MID - 1)
            def _():
                send_rear(i).wait_recv()

            @pl.when((ring < MID) | (ring == RING - 1))
            def _():
                rear_out[rows_at(i)] = rear_in[rows_at(i)] + keep_rear * total[rows_at(i)]
                send_rear(i).start()

            @pl.when(ring > last_fore)
            def _():
                finish(i, local_in[rows_at(i)] + keep_local * rear_in[rows_at(i)])

        @pl.when(active(s, lag_back))
        def _():
            i = s - lag_back
            send_back(i).wait_recv()
            spread(1 - half, i, back_in[rows_at(i)])

        @pl.when((s >= lag_join) & ((s - lag_join) % SUB == 0))
        def _():
            settle((s - lag_join) // SUB)

        return 0

    lax.fori_loop(0, lag_join + CHUNKS - SUB + 1, step, 0)

    mean = jnp.sum(squares[...], axis=-1, keepdims=True) * (1.0 / (HEADS * HD))
    scale = lax.rsqrt(mean + 1e-05)
    for h in range(HEADS):
        cols = slice(h * HD, (h + 1) * HD)
        out_ref[:, cols] = (mixed[:, cols] * scale * gain_ref[:, cols]).astype(out_ref.dtype)

    for z in range(2):
        remote(own.at[group_rows(1 - core, z)], core_in.at[pl.ds(z * OWN * HD, OWN * HD)],
               core_sent, core_got.at[0], twin).wait_send()
    remote(chip_far, chip_in, chip_sent, chip_got.at[0], across).wait_send()
    remote(back_out, back_in, back_sent, back_got.at[0], across).wait_send()
    remote(core_out, carry_in, carry_sent, carry_got.at[0], twin).wait_send()

    @pl.when(ring < last_fore)
    def _():
        remote(fore_out, fore_in, fore_sent, ring_got.at[0], ahead).wait_send()

    @pl.when((ring >= MID) & (ring < RING - 1))
    def _():
        remote(local_out, local_in, local_sent, ring_got.at[0], ahead).wait_send()

    @pl.when((ring < MID) | (ring == RING - 1))
    def _():
        remote(rear_out, rear_in, rear_sent, ring_got.at[0], behind).wait_send()


def shards(query_rows, key_rows, value_rows, seg_starts, norm_gain):
    _, tok, width = query_rows.shape
    dma = pltpu.SemaphoreType.DMA
    hbm = pl.BlockSpec(memory_space=pltpu.HBM)
    block = pltpu.VMEM((tok, width), key_rows.dtype)
    states = lambda heads: pltpu.VMEM((heads * HD, HD), F32)
    one = dma(())
    stay = lambda x: pltpu.with_memory_space_constraint(x, pltpu.HBM)
    out = pl.pallas_call(
        kernel,
        out_shape=jax.ShapeDtypeStruct((tok, width), query_rows.dtype),
        in_specs=[hbm] * 5,
        out_specs=pl.BlockSpec(memory_space=pltpu.VMEM),
        scratch_shapes=[
            pltpu.SMEM((1, 4), jnp.int32), block, block, block, pltpu.VMEM((1, width), F32),
            states(HEADS), states(2 * OWN),
            states(OWN), states(OWN), states(OWN), states(OWN),
            states(OWN), states(OWN), states(OWN), states(OWN), states(OWN), states(OWN),
            states(OWN), states(OWN), states(2 * OWN), states(2 * OWN),
            pltpu.VMEM((2 * OWN * HD, HD), jnp.bfloat16),
            pltpu.VMEM((tok, width), F32), pltpu.VMEM((tok, HD), F32),
            dma((11,)),
            one, dma((OWN + 1,)), one, dma((CHUNKS,)), one, dma((2 * CHUNKS,)),
            one, one, one, dma((CHUNKS,)), one, dma((2 * OWN,)),
        ],
        compiler_params=pltpu.CompilerParams(
            collective_id=0, has_side_effects=True, vmem_limit_bytes=32 * 1024 * 1024),
    )(stay(seg_starts), stay(query_rows[0]), stay(key_rows[0]), stay(value_rows[0]),
      stay(norm_gain.reshape(1, width)))
    return out.reshape(1, tok, width)


def solution(mesh):
    placed = (
        P("sess", "ctx", None),
        P("sess", "ctx", None),
        P("sess", "ctx", None),
        P("sess", None),
        P(),
    )
    return jax.shard_map(
        shards, mesh=mesh, in_specs=placed, out_specs=P("sess", "ctx", None), check_vma=False
    )
```

```python
import jax
import jax.numpy as jnp
from jax import lax
from jax.experimental import pallas as pl
from jax.experimental.pallas import tpu as pltpu
from jax.sharding import PartitionSpec as P

HEADS = 32
HD = 128
OWN = 8
SUB = 4
ROWS = HD // SUB
CHUNKS = OWN * SUB
RING = 8
MID = RING // 2
HOP = 8
BACK = 9
JOIN = 8
LATE = 3
DRAINED = 44
MESH = pl.DeviceIdType.MESH
F32 = jnp.float32


def rows_at(i):
    return pl.ds(pl.multiple_of(i * ROWS, ROWS), ROWS)


def head_rows(n):
    return pl.ds(pl.multiple_of(n * HD, HD), HD)


def head_cols(h):
    return pl.ds(pl.multiple_of(h * HD, HD), HD)


def kernel(starts_hbm, q_hbm, k_hbm, v_hbm, gain_hbm, out_ref,
           starts, q_ref, k_ref, v_ref, gain_ref,
           own, core_in, chip_far, chip_own, chip_in, total,
           fore_out, fore_in, local_out, local_in, rear_out, rear_in,
           back_out, back_in, core_out, carry_in, carry, mixed, squares,
           loads, core_sent, core_got, chip_sent, chip_got, fore_sent, ring_got,
           local_sent, rear_sent, back_sent, back_got, carry_sent, carry_got):
    me = lax.axis_index("ctx")
    core = me % 2
    half = (me // 2) % 2
    ring = me // 4
    tok = q_ref.shape[0]
    base = me * tok

    twin = {"ctx": me + 1 - 2 * core}
    across = {"ctx": me + 2 - 4 * half}
    ahead = {"ctx": (me + 4) % (4 * RING)}
    behind = {"ctx": (me + 4 * RING - 4) % (4 * RING)}

    last_fore = MID + 1

    def group(c, z):
        return (2 * c + z) * OWN

    def group_rows(c, z):
        return pl.ds(pl.multiple_of(group(c, z) * HD, HD), OWN * HD)

    order = [(1 - core, 1 - half), (core, 1 - half), (1 - core, half), (core, half)]
    fetch_starts = pltpu.make_async_copy(starts_hbm, starts, loads.at[0])
    fetch_keys = [pltpu.make_async_copy(
        k_hbm.at[:, group_rows(*g)], k_ref.at[:, group_rows(*g)], loads.at[1 + n]) for n, g in enumerate(order)]
    fetch_values = [pltpu.make_async_copy(
        v_hbm.at[:, group_rows(*g)], v_ref.at[:, group_rows(*g)], loads.at[5 + n]) for n, g in enumerate(order)]
    fetch_rest = [pltpu.make_async_copy(q_hbm, q_ref, loads.at[9]),
                  pltpu.make_async_copy(gain_hbm, gain_ref, loads.at[10])]
    fetch_starts.start()
    fetch_keys[0].start()
    fetch_values[0].start()
    barrier = pltpu.get_barrier_semaphore()

    def greet(other):
        pl.semaphore_signal(barrier, inc=1, device_id=other, device_id_type=MESH)

    def rear_lands(place):
        return (place == 1) | (place == 2) | (place >= RING - 2)

    greet(twin)
    greet(across)

    @pl.when(ring > 0)
    def _():
        greet(behind)

    @pl.when(rear_lands(ring))
    def _():
        greet(ahead)

    for n in range(1, 4):
        fetch_keys[n].start()
        fetch_values[n].start()
    for fetch in fetch_rest:
        fetch.start()
    fetch_starts.wait()

    start = [starts[0, n] for n in range(4)]

    def keep(low, size):
        inside = [jnp.where((s >= low) & (s < low + size), 1, 0) for s in start]
        return jnp.where(sum(inside) == 0, 1.0, 0.0).astype(F32)

    chip_base = (me // 2) * (2 * tok)
    span = 4 * tok
    ring_base = ring * span
    keep_core0 = keep(chip_base, tok)
    keep_core1 = keep(chip_base + tok, tok)
    keep_chip0 = keep(ring_base, 2 * tok)
    keep_chip1 = keep(ring_base + 2 * tok, 2 * tok)
    keep_ring = keep(ring_base, span)
    keep_local = keep(MID * span, ring_base - MID * span)
    one, nil = jnp.float32(1.0), jnp.float32(0.0)
    keep_rear = jnp.where(ring >= MID, nil, keep(ring_base + span, (MID - 1 - ring) * span))
    first_core, first_half = core == 0, half == 0
    a_own = jnp.where(first_core, keep_core1, one)
    a_in = jnp.where(first_core, one, keep_core1)
    b_own = jnp.where(first_half, keep_chip1, one)
    b_in = jnp.where(first_half, one, keep_chip1)
    e_own, e_scan = jnp.where(first_half, one, nil), jnp.where(first_half, keep_chip0, one)
    p_in, p_scan = jnp.where(first_half, nil, one), jnp.where(first_half, one, keep_chip0)
    f_own, f_pre = jnp.where(first_core, one, nil), jnp.where(first_core, keep_core0, one)
    g_in, g_pre = jnp.where(first_core, nil, one), jnp.where(first_core, one, keep_core0)

    def segment(pos):
        return sum((s <= pos).astype(jnp.int32) for s in start)

    row = lax.broadcasted_iota(jnp.int32, (tok, 1), 0) + base
    col = lax.broadcasted_iota(jnp.int32, (1, tok), 1) + base
    seg_row, seg_col = segment(row), segment(col)
    prior = sum(jnp.where(s < base, 1, 0) for s in start)
    last = sum(jnp.where(s < base + tok, 1, 0) for s in start)
    use = jnp.where(seg_row == prior, 1.0, 0.0).astype(F32)
    allowed = (row >= col) & (seg_row == seg_col)
    keep_rows = jnp.where(seg_row == last, 1.0, 0.0).astype(k_ref.dtype)

    def remote(src, dst, sent, got, device):
        return pltpu.make_async_remote_copy(
            src_ref=src, dst_ref=dst, send_sem=sent, recv_sem=got,
            device_id=device, device_id_type=MESH)

    def send_core(j):
        z = 1 - half
        return remote(own.at[head_rows(group(1 - core, z) + j)], core_in.at[head_rows(z * OWN + j)],
                      core_sent, core_got.at[j], twin)

    def send_rest():
        return remote(own.at[group_rows(1 - core, half)], core_in.at[pl.ds(half * OWN * HD, OWN * HD)],
                      core_sent, core_got.at[OWN], twin)

    def send_chip(i):
        return remote(chip_far.at[rows_at(i)], chip_in.at[rows_at(i)],
                      chip_sent, chip_got.at[i], across)

    def send_fore(i):
        return remote(fore_out.at[rows_at(i)], fore_in.at[rows_at(i)],
                      fore_sent, ring_got.at[i], ahead)

    def local_lane(place):
        return jnp.where(place == last_fore, CHUNKS, 0)

    def send_local(i, place):
        return remote(local_out.at[rows_at(i)], local_in.at[rows_at(i)],
                      local_sent, ring_got.at[local_lane(place) + i], ahead)

    def send_rear(i):
        return remote(rear_out.at[rows_at(i)], rear_in.at[rows_at(i)],
                      rear_sent, ring_got.at[CHUNKS + i], behind)

    def send_back(i):
        return remote(back_out.at[rows_at(i)], back_in.at[rows_at(i)],
                      back_sent, back_got.at[i], across)

    def send_carry(n):
        return remote(core_out.at[head_rows(n)], carry_in.at[head_rows(n)],
                      carry_sent, carry_got.at[n], twin)

    def summaries(n):
        fetch_keys[n].wait()
        fetch_values[n].wait()
        first = group(*order[n])
        states = []
        for j in range(OWN):
            cols = head_cols(first + j)
            states.append(lax.dot_general(
                k_ref[:, cols] * keep_rows, v_ref[:, cols],
                (((0,), (0,)), ((), ())), preferred_element_type=F32))
        for j in range(OWN):
            own[head_rows(first + j)] = states[j]

    summaries(0)
    greeted = jnp.where(ring < RING - 1, 1, 0) + jnp.where(rear_lands((ring + RING - 1) % RING), 1, 0)
    pl.semaphore_wait(barrier, 2 + greeted)
    for j in range(OWN):
        send_core(j).start()
    summaries(1)

    def chip_total(z, j):
        return a_own * own[head_rows(group(core, z) + j)] + a_in * core_in[head_rows(z * OWN + j)]

    def far(j, _):
        send_core(j).wait_recv()
        chip_far[head_rows(j)] = chip_total(1 - half, j)
        for s in range(SUB):
            send_chip(j * SUB + s).start()
        return 0

    def near(j, _):
        chip_own[head_rows(j)] = chip_total(half, j)
        return 0

    lax.fori_loop(0, OWN, far, 0)
    summaries(2)
    send_rest().start()
    summaries(3)

    @pl.when(ring == 0)
    def _():
        fore_in[...] = jnp.zeros_like(fore_in)

    @pl.when(ring == MID)
    def _():
        local_in[...] = jnp.zeros_like(local_in)

    @pl.when(ring == MID - 1)
    def _():
        rear_in[...] = jnp.zeros_like(rear_in)

    def intra(n, _):
        cols = [head_cols(n * 8 + m) for m in range(8)]
        scores = [lax.dot_general(
            q_ref[:, c], k_ref[:, c], (((1,), (1,)), ((), ())), preferred_element_type=F32)
            for c in cols]
        weights = [jnp.where(allowed, s, 0.0).astype(v_ref.dtype) for s in scores]
        values = [jnp.dot(w, v_ref[:, c], preferred_element_type=F32) for w, c in zip(weights, cols)]
        for c, value in zip(cols, values):
            mixed[:, c] = value
        return 0

    for fetch in fetch_rest:
        fetch.wait()
    squares[...] = jnp.zeros_like(squares)
    lax.fori_loop(0, HEADS // 8, intra, 0)
    send_rest().wait_recv()
    lax.fori_loop(0, OWN, near, 0)

    def spread(z, i, prefix):
        n = z * CHUNKS + i
        core_out[rows_at(n)] = f_own * own[rows_at(group(core, z) * SUB + i)] + f_pre * prefix
        carry[rows_at(n)] = (g_in * core_in[rows_at(n)] + g_pre * prefix).astype(carry.dtype)

        @pl.when(i % SUB == SUB - 1)
        def _():
            send_carry(z * OWN + i // SUB).start()

    def finish(i, prefix):
        arrived, mine = chip_in[rows_at(i)], chip_own[rows_at(i)]
        back_out[rows_at(i)] = e_own * mine + e_scan * prefix
        send_back(i).start()
        spread(half, i, p_in * arrived + p_scan * prefix)

    lag_local = HOP * (ring - MID)
    late = jnp.where(lax.axis_index("sess") == 0, LATE, 0)
    lag_fore = HOP * ring + jnp.where(ring == 0, 0, late)
    lag_rear = HOP * ((RING + MID - 1 - ring) % RING) - jnp.where(ring == 0, late, 0)
    ends = (ring > MID) & (ring < RING - 1)
    lag_prefix = jnp.where(ring <= last_fore, lag_fore, lag_rear)
    lag_back = jnp.where(ends, lag_prefix + BACK, jnp.maximum(lag_prefix + 2 * BACK, DRAINED))
    lag_join = lag_back + SUB + JOIN

    def settle(j):
        heads, states = [], []
        for z in (half, 1 - half):
            heads.append(group(core, z) + j)
            states.append(carry[head_rows(z * OWN + j)])
        for z in (half, 1 - half):
            send_carry(z * OWN + j).wait_recv()
            heads.append(group(1 - core, z) + j)
            states.append(carry_in[head_rows(z * OWN + j)].astype(carry.dtype))
        cols = [head_cols(h) for h in heads]
        inter = [jnp.dot(q_ref[:, c], state, preferred_element_type=F32) for c, state in zip(cols, states)]
        values = [mixed[:, c] + use * part for c, part in zip(cols, inter)]
        for c, value in zip(cols, values):
            mixed[:, c] = value
        squares[...] += sum(value * value for value in values)

    def active(s, lag):
        return (s >= lag) & (s < lag + CHUNKS)

    def step(s, _):
        @pl.when(s < CHUNKS)
        def _():
            send_chip(s).wait_recv()
            total[rows_at(s)] = b_own * chip_own[rows_at(s)] + b_in * chip_in[rows_at(s)]

        @pl.when((ring >= MID) & active(s, lag_local))
        def _():
            i = s - lag_local

            @pl.when(ring > MID)
            def _():
                send_local(i, ring).wait_recv()

            @pl.when(ring < RING - 1)
            def _():
                local_out[rows_at(i)] = total[rows_at(i)] + keep_ring * local_in[rows_at(i)]
                send_local(i, ring + 1).start()

        @pl.when((ring <= last_fore) & active(s, lag_fore))
        def _():
            i = s - lag_fore

            @pl.when(ring > 0)
            def _():
                send_fore(i).wait_recv()

            prefix = fore_in[rows_at(i)]

            @pl.when(ring < last_fore)
            def _():
                fore_out[rows_at(i)] = total[rows_at(i)] + keep_ring * prefix
                send_fore(i).start()

            finish(i, prefix)

        @pl.when(((ring < MID) | (ring > last_fore)) & active(s, lag_rear))
        def _():
            i = s - lag_rear

            @pl.when(ring != MID - 1)
            def _():
                send_rear(i).wait_recv()

            @pl.when((ring < MID) | (ring == RING - 1))
            def _():
                rear_out[rows_at(i)] = rear_in[rows_at(i)] + keep_rear * total[rows_at(i)]
                send_rear(i).start()

            @pl.when(ring > last_fore)
            def _():
                finish(i, local_in[rows_at(i)] + keep_local * rear_in[rows_at(i)])

        @pl.when(active(s, lag_back))
        def _():
            i = s - lag_back
            send_back(i).wait_recv()
            spread(1 - half, i, back_in[rows_at(i)])

        @pl.when((s >= lag_join) & ((s - lag_join) % SUB == 0))
        def _():
            settle((s - lag_join) // SUB)

        return 0

    lax.fori_loop(0, lag_join + CHUNKS - SUB + 1, step, 0)

    mean = jnp.sum(squares[...], axis=-1, keepdims=True) * (1.0 / (HEADS * HD))
    scale = lax.rsqrt(mean + 1e-05)
    for h in range(HEADS):
        cols = slice(h * HD, (h + 1) * HD)
        out_ref[:, cols] = (mixed[:, cols] * scale * gain_ref[:, cols]).astype(out_ref.dtype)

    for z in range(2):
        remote(own.at[group_rows(1 - core, z)], core_in.at[pl.ds(z * OWN * HD, OWN * HD)],
               core_sent, core_got.at[0], twin).wait_send()
    remote(chip_far, chip_in, chip_sent, chip_got.at[0], across).wait_send()
    remote(back_out, back_in, back_sent, back_got.at[0], across).wait_send()
    remote(core_out, carry_in, carry_sent, carry_got.at[0], twin).wait_send()

    @pl.when(ring < last_fore)
    def _():
        remote(fore_out, fore_in, fore_sent, ring_got.at[0], ahead).wait_send()

    @pl.when((ring >= MID) & (ring < RING - 1))
    def _():
        remote(local_out, local_in, local_sent, ring_got.at[0], ahead).wait_send()

    @pl.when((ring < MID) | (ring == RING - 1))
    def _():
        remote(rear_out, rear_in, rear_sent, ring_got.at[0], behind).wait_send()


def shards(query_rows, key_rows, value_rows, seg_starts, norm_gain):
    _, tok, width = query_rows.shape
    dma = pltpu.SemaphoreType.DMA
    hbm = pl.BlockSpec(memory_space=pltpu.HBM)
    block = pltpu.VMEM((tok, width), key_rows.dtype)
    states = lambda heads: pltpu.VMEM((heads * HD, HD), F32)
    one = dma(())
    stay = lambda x: pltpu.with_memory_space_constraint(x, pltpu.HBM)
    out = pl.pallas_call(
        kernel,
        out_shape=jax.ShapeDtypeStruct((tok, width), query_rows.dtype),
        in_specs=[hbm] * 5,
        out_specs=pl.BlockSpec(memory_space=pltpu.VMEM),
        scratch_shapes=[
            pltpu.SMEM((1, 4), jnp.int32), block, block, block, pltpu.VMEM((1, width), F32),
            states(HEADS), states(2 * OWN),
            states(OWN), states(OWN), states(OWN), states(OWN),
            states(OWN), states(OWN), states(OWN), states(OWN), states(OWN), states(OWN),
            states(OWN), states(OWN), states(2 * OWN), states(2 * OWN),
            pltpu.VMEM((2 * OWN * HD, HD), jnp.bfloat16),
            pltpu.VMEM((tok, width), F32), pltpu.VMEM((tok, HD), F32),
            dma((11,)),
            one, dma((OWN + 1,)), one, dma((CHUNKS,)), one, dma((2 * CHUNKS,)),
            one, one, one, dma((CHUNKS,)), one, dma((2 * OWN,)),
        ],
        compiler_params=pltpu.CompilerParams(
            collective_id=0, has_side_effects=True, vmem_limit_bytes=32 * 1024 * 1024),
    )(stay(seg_starts), stay(query_rows[0]), stay(key_rows[0]), stay(value_rows[0]),
      stay(norm_gain.reshape(1, width)))
    return out.reshape(1, tok, width)


def solution(mesh):
    placed = (
        P("sess", "ctx", None),
        P("sess", "ctx", None),
        P("sess", "ctx", None),
        P("sess", None),
        P(),
    )
    return jax.shard_map(
        shards, mesh=mesh, in_specs=placed, out_specs=P("sess", "ctx", None), check_vma=False
    )
```

```python
import jax
import jax.numpy as jnp
from jax import lax
from jax.experimental import pallas as pl
from jax.experimental.pallas import tpu as pltpu
from jax.sharding import PartitionSpec as P

HEADS = 32
HD = 128
OWN = 8
SUB = 4
ROWS = HD // SUB
CHUNKS = OWN * SUB
RING = 8
MID = RING // 2
HOP = 8
BACK = 9
JOIN = 8
LATE = 3
DRAINED = 44
MESH = pl.DeviceIdType.MESH
F32 = jnp.float32


def rows_at(i):
    return pl.ds(pl.multiple_of(i * ROWS, ROWS), ROWS)


def head_rows(n):
    return pl.ds(pl.multiple_of(n * HD, HD), HD)


def head_cols(h):
    return pl.ds(pl.multiple_of(h * HD, HD), HD)


def kernel(starts_hbm, q_hbm, k_hbm, v_hbm, gain_hbm, out_ref,
           starts, q_ref, k_ref, v_ref, gain_ref,
           own, core_in, chip_far, chip_own, chip_in, total,
           fore_out, fore_in, local_out, local_in, rear_out, rear_in,
           back_out, back_in, core_out, carry_in, carry, mixed, squares,
           loads, core_sent, chip_sent, fore_sent,
           local_sent, rear_sent, back_sent, back_got, carry_sent, carry_got):
    me = lax.axis_index("ctx")
    core = me % 2
    half = (me // 2) % 2
    ring = me // 4
    tok = q_ref.shape[0]
    base = me * tok

    twin = {"ctx": me + 1 - 2 * core}
    across = {"ctx": me + 2 - 4 * half}
    ahead = {"ctx": (me + 4) % (4 * RING)}
    behind = {"ctx": (me + 4 * RING - 4) % (4 * RING)}

    last_fore = MID + 1

    def group(c, z):
        return (2 * c + z) * OWN

    def group_rows(c, z):
        return pl.ds(pl.multiple_of(group(c, z) * HD, HD), OWN * HD)

    order = [(1 - core, 1 - half), (core, 1 - half), (1 - core, half), (core, half)]
    fetch_starts = pltpu.make_async_copy(starts_hbm, starts, loads.at[0])
    fetch_keys = [pltpu.make_async_copy(
        k_hbm.at[:, group_rows(*g)], k_ref.at[:, group_rows(*g)], loads.at[1 + n]) for n, g in enumerate(order)]
    fetch_values = [pltpu.make_async_copy(
        v_hbm.at[:, group_rows(*g)], v_ref.at[:, group_rows(*g)], loads.at[5 + n]) for n, g in enumerate(order)]
    fetch_rest = [pltpu.make_async_copy(q_hbm, q_ref, loads.at[9]),
                  pltpu.make_async_copy(gain_hbm, gain_ref, loads.at[10])]
    def remote(src, dst, sent, got, device):
        return pltpu.make_async_remote_copy(
            src_ref=src, dst_ref=dst, send_sem=sent, recv_sem=got,
            device_id=device, device_id_type=MESH)

    def phase(first, core_got=None, chip_got=None, ring_got=None):
        if first:
            fetch_starts.start()
            fetch_keys[0].start()
            fetch_values[0].start()
            barrier = pltpu.get_barrier_semaphore()

            def greet(other):
                pl.semaphore_signal(barrier, inc=1, device_id=other, device_id_type=MESH)

            def rear_lands(place):
                return (place == 1) | (place == 2) | (place >= RING - 2)

            greet(twin)
            greet(across)

            @pl.when(ring > 0)
            def _():
                greet(behind)

            @pl.when(rear_lands(ring))
            def _():
                greet(ahead)

            for n in range(1, 4):
                fetch_keys[n].start()
                fetch_values[n].start()
            for fetch in fetch_rest:
                fetch.start()
            fetch_starts.wait()

        start = [starts[0, n] for n in range(4)]

        def keep(low, size):
            inside = [jnp.where((s >= low) & (s < low + size), 1, 0) for s in start]
            return jnp.where(sum(inside) == 0, 1.0, 0.0).astype(F32)

        chip_base = (me // 2) * (2 * tok)
        span = 4 * tok
        ring_base = ring * span
        keep_core0 = keep(chip_base, tok)
        keep_core1 = keep(chip_base + tok, tok)
        keep_chip0 = keep(ring_base, 2 * tok)
        keep_chip1 = keep(ring_base + 2 * tok, 2 * tok)
        keep_ring = keep(ring_base, span)
        keep_local = keep(MID * span, ring_base - MID * span)
        one, nil = jnp.float32(1.0), jnp.float32(0.0)
        keep_rear = jnp.where(ring >= MID, nil, keep(ring_base + span, (MID - 1 - ring) * span))
        first_core, first_half = core == 0, half == 0
        a_own = jnp.where(first_core, keep_core1, one)
        a_in = jnp.where(first_core, one, keep_core1)
        b_own = jnp.where(first_half, keep_chip1, one)
        b_in = jnp.where(first_half, one, keep_chip1)
        e_own, e_scan = jnp.where(first_half, one, nil), jnp.where(first_half, keep_chip0, one)
        p_in, p_scan = jnp.where(first_half, nil, one), jnp.where(first_half, one, keep_chip0)
        f_own, f_pre = jnp.where(first_core, one, nil), jnp.where(first_core, keep_core0, one)
        g_in, g_pre = jnp.where(first_core, nil, one), jnp.where(first_core, one, keep_core0)

        def segment(pos):
            return sum((s <= pos).astype(jnp.int32) for s in start)

        row = lax.broadcasted_iota(jnp.int32, (tok, 1), 0) + base
        col = lax.broadcasted_iota(jnp.int32, (1, tok), 1) + base
        seg_row, seg_col = segment(row), segment(col)
        prior = sum(jnp.where(s < base, 1, 0) for s in start)
        last = sum(jnp.where(s < base + tok, 1, 0) for s in start)
        use = jnp.where(seg_row == prior, 1.0, 0.0).astype(F32)
        allowed = (row >= col) & (seg_row == seg_col)
        keep_rows = jnp.where(seg_row == last, 1.0, 0.0).astype(k_ref.dtype)

        def send_core(j):
            z = 1 - half
            return remote(own.at[head_rows(group(1 - core, z) + j)], core_in.at[head_rows(z * OWN + j)],
                          core_sent, core_got.at[j], twin)

        def send_rest():
            return remote(own.at[group_rows(1 - core, half)], core_in.at[pl.ds(half * OWN * HD, OWN * HD)],
                          core_sent, core_got.at[OWN], twin)

        def send_chip(i):
            return remote(chip_far.at[rows_at(i)], chip_in.at[rows_at(i)],
                          chip_sent, chip_got.at[i], across)

        def send_fore(i):
            return remote(fore_out.at[rows_at(i)], fore_in.at[rows_at(i)],
                          fore_sent, ring_got.at[i], ahead)

        def local_lane(place):
            return jnp.where(place == last_fore, CHUNKS, 0)

        def send_local(i, place):
            return remote(local_out.at[rows_at(i)], local_in.at[rows_at(i)],
                          local_sent, ring_got.at[local_lane(place) + i], ahead)

        def send_rear(i):
            return remote(rear_out.at[rows_at(i)], rear_in.at[rows_at(i)],
                          rear_sent, ring_got.at[CHUNKS + i], behind)

        def send_back(i):
            return remote(back_out.at[rows_at(i)], back_in.at[rows_at(i)],
                          back_sent, back_got.at[i], across)

        def send_carry(n):
            return remote(core_out.at[head_rows(n)], carry_in.at[head_rows(n)],
                          carry_sent, carry_got.at[n], twin)

        def summaries(n):
            fetch_keys[n].wait()
            fetch_values[n].wait()
            first = group(*order[n])
            states = []
            for j in range(OWN):
                cols = head_cols(first + j)
                states.append(lax.dot_general(
                    k_ref[:, cols] * keep_rows, v_ref[:, cols],
                    (((0,), (0,)), ((), ())), preferred_element_type=F32))
            for j in range(OWN):
                own[head_rows(first + j)] = states[j]

        if first:
            summaries(0)
            greeted = jnp.where(ring < RING - 1, 1, 0) + jnp.where(rear_lands((ring + RING - 1) % RING), 1, 0)
            pl.semaphore_wait(barrier, 2 + greeted)
            for j in range(OWN):
                send_core(j).start()
            summaries(1)

        def chip_total(z, j):
            return a_own * own[head_rows(group(core, z) + j)] + a_in * core_in[head_rows(z * OWN + j)]

        def far(j, _):
            send_core(j).wait_recv()
            chip_far[head_rows(j)] = chip_total(1 - half, j)
            for s in range(SUB):
                send_chip(j * SUB + s).start()
            return 0

        def near(j, _):
            chip_own[head_rows(j)] = chip_total(half, j)
            return 0

        if first:
            lax.fori_loop(0, OWN, far, 0)
            summaries(2)
            send_rest().start()
            summaries(3)

            @pl.when(ring == 0)
            def _():
                fore_in[...] = jnp.zeros_like(fore_in)

            @pl.when(ring == MID)
            def _():
                local_in[...] = jnp.zeros_like(local_in)

            @pl.when(ring == MID - 1)
            def _():
                rear_in[...] = jnp.zeros_like(rear_in)

        def intra(n, _):
            cols = [head_cols(n * 8 + m) for m in range(8)]
            scores = [lax.dot_general(
                q_ref[:, c], k_ref[:, c], (((1,), (1,)), ((), ())), preferred_element_type=F32)
                for c in cols]
            weights = [jnp.where(allowed, s, 0.0).astype(v_ref.dtype) for s in scores]
            values = [jnp.dot(w, v_ref[:, c], preferred_element_type=F32) for w, c in zip(weights, cols)]
            for c, value in zip(cols, values):
                mixed[:, c] = value
            return 0

        if first:
            for fetch in fetch_rest:
                fetch.wait()
            squares[...] = jnp.zeros_like(squares)
            lax.fori_loop(0, HEADS // 8, intra, 0)
            send_rest().wait_recv()
            lax.fori_loop(0, OWN, near, 0)

        def spread(z, i, prefix):
            n = z * CHUNKS + i
            core_out[rows_at(n)] = f_own * own[rows_at(group(core, z) * SUB + i)] + f_pre * prefix
            carry[rows_at(n)] = (g_in * core_in[rows_at(n)] + g_pre * prefix).astype(carry.dtype)

            @pl.when(i % SUB == SUB - 1)
            def _():
                send_carry(z * OWN + i // SUB).start()

        def finish(i, prefix):
            arrived, mine = chip_in[rows_at(i)], chip_own[rows_at(i)]
            back_out[rows_at(i)] = e_own * mine + e_scan * prefix
            send_back(i).start()
            spread(half, i, p_in * arrived + p_scan * prefix)

        lag_local = HOP * (ring - MID)
        late = jnp.where(lax.axis_index("sess") == 0, LATE, 0)
        lag_fore = HOP * ring + jnp.where(ring == 0, 0, late)
        lag_rear = HOP * ((RING + MID - 1 - ring) % RING) - jnp.where(ring == 0, late, 0)
        ends = (ring > MID) & (ring < RING - 1)
        lag_prefix = jnp.where(ring <= last_fore, lag_fore, lag_rear)
        lag_back = jnp.where(ends, lag_prefix + BACK, jnp.maximum(lag_prefix + 2 * BACK, DRAINED))
        lag_join = lag_back + SUB + JOIN

        def settle(j):
            heads, states = [], []
            for z in (half, 1 - half):
                heads.append(group(core, z) + j)
                states.append(carry[head_rows(z * OWN + j)])
            for z in (half, 1 - half):
                send_carry(z * OWN + j).wait_recv()
                heads.append(group(1 - core, z) + j)
                states.append(carry_in[head_rows(z * OWN + j)].astype(carry.dtype))
            cols = [head_cols(h) for h in heads]
            inter = [jnp.dot(q_ref[:, c], state, preferred_element_type=F32) for c, state in zip(cols, states)]
            values = [mixed[:, c] + use * part for c, part in zip(cols, inter)]
            for c, value in zip(cols, values):
                mixed[:, c] = value
            squares[...] += sum(value * value for value in values)

        def active(s, lag):
            return (s >= lag) & (s < lag + CHUNKS)

        def step(s, _):
            if first:
                @pl.when(s < CHUNKS)
                def _():
                    send_chip(s).wait_recv()
                    total[rows_at(s)] = b_own * chip_own[rows_at(s)] + b_in * chip_in[rows_at(s)]

                @pl.when((ring >= MID) & active(s, lag_local))
                def _():
                    i = s - lag_local

                    @pl.when(ring > MID)
                    def _():
                        send_local(i, ring).wait_recv()

                    @pl.when(ring < RING - 1)
                    def _():
                        local_out[rows_at(i)] = total[rows_at(i)] + keep_ring * local_in[rows_at(i)]
                        send_local(i, ring + 1).start()

                @pl.when((ring <= last_fore) & active(s, lag_fore))
                def _():
                    i = s - lag_fore

                    @pl.when(ring > 0)
                    def _():
                        send_fore(i).wait_recv()

                    prefix = fore_in[rows_at(i)]

                    @pl.when(ring < last_fore)
                    def _():
                        fore_out[rows_at(i)] = total[rows_at(i)] + keep_ring * prefix
                        send_fore(i).start()

                    finish(i, prefix)

                @pl.when(((ring < MID) | (ring > last_fore)) & active(s, lag_rear))
                def _():
                    i = s - lag_rear

                    @pl.when(ring != MID - 1)
                    def _():
                        send_rear(i).wait_recv()

                    @pl.when((ring < MID) | (ring == RING - 1))
                    def _():
                        rear_out[rows_at(i)] = rear_in[rows_at(i)] + keep_rear * total[rows_at(i)]
                        send_rear(i).start()

                    @pl.when(ring > last_fore)
                    def _():
                        finish(i, local_in[rows_at(i)] + keep_local * rear_in[rows_at(i)])

            @pl.when(active(s, lag_back))
            def _():
                i = s - lag_back
                send_back(i).wait_recv()
                spread(1 - half, i, back_in[rows_at(i)])

            @pl.when((s >= lag_join) & ((s - lag_join) % SUB == 0))
            def _():
                settle((s - lag_join) // SUB)

            return 0

        streamed = CHUNKS + jnp.maximum(
            jnp.where(ring <= last_fore, lag_fore, 0),
            jnp.where((ring < MID) | (ring > last_fore), lag_rear, 0))
        if first:
            lax.fori_loop(0, streamed, step, 0)
        else:
            lax.fori_loop(streamed, lag_join + CHUNKS - SUB + 1, step, 0)

    pl.run_scoped(
        lambda *got: phase(True, *got),
        pltpu.SemaphoreType.DMA((OWN + 1,)), pltpu.SemaphoreType.DMA((CHUNKS,)), pltpu.SemaphoreType.DMA((2 * CHUNKS,)))
    phase(False)
    mean = jnp.sum(squares[...], axis=-1, keepdims=True) * (1.0 / (HEADS * HD))
    scale = lax.rsqrt(mean + 1e-05)
    for h in range(HEADS):
        cols = slice(h * HD, (h + 1) * HD)
        out_ref[:, cols] = (mixed[:, cols] * scale * gain_ref[:, cols]).astype(out_ref.dtype)

    for z in range(2):
        remote(own.at[group_rows(1 - core, z)], core_in.at[pl.ds(z * OWN * HD, OWN * HD)],
               core_sent, back_got.at[0], twin).wait_send()
    remote(chip_far, chip_in, chip_sent, back_got.at[0], across).wait_send()
    remote(back_out, back_in, back_sent, back_got.at[0], across).wait_send()
    remote(core_out, carry_in, carry_sent, carry_got.at[0], twin).wait_send()

    @pl.when(ring < last_fore)
    def _():
        remote(fore_out, fore_in, fore_sent, back_got.at[0], ahead).wait_send()

    @pl.when((ring >= MID) & (ring < RING - 1))
    def _():
        remote(local_out, local_in, local_sent, back_got.at[0], ahead).wait_send()

    @pl.when((ring < MID) | (ring == RING - 1))
    def _():
        remote(rear_out, rear_in, rear_sent, back_got.at[0], behind).wait_send()


def shards(query_rows, key_rows, value_rows, seg_starts, norm_gain):
    _, tok, width = query_rows.shape
    dma = pltpu.SemaphoreType.DMA
    hbm = pl.BlockSpec(memory_space=pltpu.HBM)
    block = pltpu.VMEM((tok, width), key_rows.dtype)
    states = lambda heads: pltpu.VMEM((heads * HD, HD), F32)
    one = dma(())
    stay = lambda x: pltpu.with_memory_space_constraint(x, pltpu.HBM)
    out = pl.pallas_call(
        kernel,
        out_shape=jax.ShapeDtypeStruct((tok, width), query_rows.dtype),
        in_specs=[hbm] * 5,
        out_specs=pl.BlockSpec(memory_space=pltpu.VMEM),
        scratch_shapes=[
            pltpu.SMEM((1, 4), jnp.int32), block, block, block, pltpu.VMEM((1, width), F32),
            states(HEADS), states(2 * OWN),
            states(OWN), states(OWN), states(OWN), states(OWN),
            states(OWN), states(OWN), states(OWN), states(OWN), states(OWN), states(OWN),
            states(OWN), states(OWN), states(2 * OWN), states(2 * OWN),
            pltpu.VMEM((2 * OWN * HD, HD), jnp.bfloat16),
            pltpu.VMEM((tok, width), F32), pltpu.VMEM((tok, HD), F32),
            dma((11,)),
            one, one, one, one, one, one, dma((CHUNKS,)), one, dma((2 * OWN,)),
        ],
        compiler_params=pltpu.CompilerParams(
            collective_id=0, has_side_effects=True, vmem_limit_bytes=32 * 1024 * 1024),
    )(stay(seg_starts), stay(query_rows[0]), stay(key_rows[0]), stay(value_rows[0]),
      stay(norm_gain.reshape(1, width)))
    return out.reshape(1, tok, width)


def solution(mesh):
    placed = (
        P("sess", "ctx", None),
        P("sess", "ctx", None),
        P("sess", "ctx", None),
        P("sess", None),
        P(),
    )
    return jax.shard_map(
        shards, mesh=mesh, in_specs=placed, out_specs=P("sess", "ctx", None), check_vma=False
    )
```

```python
import jax
import jax.numpy as jnp
from jax import lax
from jax.experimental import pallas as pl
from jax.experimental.pallas import tpu as pltpu
from jax.sharding import PartitionSpec as P

HEADS = 32
HD = 128
OWN = 8
SUB = 8
ROWS = HD // SUB
CHUNKS = OWN * SUB
RING = 8
MID = RING // 2
HOP = 16
BACK = 17
JOIN = 14
LATE = 6
DRAINED = 86
MESH = pl.DeviceIdType.MESH
F32 = jnp.float32


def rows_at(i):
    return pl.ds(pl.multiple_of(i * ROWS, ROWS), ROWS)


def head_rows(n):
    return pl.ds(pl.multiple_of(n * HD, HD), HD)


def head_cols(h):
    return pl.ds(pl.multiple_of(h * HD, HD), HD)


def kernel(starts_hbm, q_hbm, k_hbm, v_hbm, gain_hbm, out_ref,
           starts, q_ref, k_ref, v_ref, gain_ref,
           own, core_in, chip_far, chip_own, chip_in, total,
           fore_out, fore_in, local_out, local_in, rear_out, rear_in,
           back_out, back_in, core_out, carry_in, carry, mixed, squares,
           loads, core_sent, chip_sent, fore_sent,
           local_sent, rear_sent, back_sent, back_got, carry_sent, carry_got):
    me = lax.axis_index("ctx")
    core = me % 2
    half = (me // 2) % 2
    ring = me // 4
    tok = q_ref.shape[0]
    base = me * tok

    twin = {"ctx": me + 1 - 2 * core}
    across = {"ctx": me + 2 - 4 * half}
    ahead = {"ctx": (me + 4) % (4 * RING)}
    behind = {"ctx": (me + 4 * RING - 4) % (4 * RING)}

    last_fore = MID + 1

    def group(c, z):
        return (2 * c + z) * OWN

    def group_rows(c, z):
        return pl.ds(pl.multiple_of(group(c, z) * HD, HD), OWN * HD)

    order = [(1 - core, 1 - half), (core, 1 - half), (1 - core, half), (core, half)]
    fetch_starts = pltpu.make_async_copy(starts_hbm, starts, loads.at[0])
    fetch_keys = [pltpu.make_async_copy(
        k_hbm.at[:, group_rows(*g)], k_ref.at[:, group_rows(*g)], loads.at[1 + n]) for n, g in enumerate(order)]
    fetch_values = [pltpu.make_async_copy(
        v_hbm.at[:, group_rows(*g)], v_ref.at[:, group_rows(*g)], loads.at[5 + n]) for n, g in enumerate(order)]
    fetch_rest = [pltpu.make_async_copy(q_hbm, q_ref, loads.at[9]),
                  pltpu.make_async_copy(gain_hbm, gain_ref, loads.at[10])]
    def remote(src, dst, sent, got, device):
        return pltpu.make_async_remote_copy(
            src_ref=src, dst_ref=dst, send_sem=sent, recv_sem=got,
            device_id=device, device_id_type=MESH)

    def phase(first, core_got=None, chip_got=None, ring_got=None):
        if first:
            fetch_starts.start()
            fetch_keys[0].start()
            fetch_values[0].start()
            barrier = pltpu.get_barrier_semaphore()

            def greet(other):
                pl.semaphore_signal(barrier, inc=1, device_id=other, device_id_type=MESH)

            def rear_lands(place):
                return (place == 1) | (place == 2) | (place >= RING - 2)

            greet(twin)
            greet(across)

            @pl.when(ring > 0)
            def _():
                greet(behind)

            @pl.when(rear_lands(ring))
            def _():
                greet(ahead)

            for n in range(1, 4):
                fetch_keys[n].start()
                fetch_values[n].start()
            for fetch in fetch_rest:
                fetch.start()
            fetch_starts.wait()

        start = [starts[0, n] for n in range(4)]

        def keep(low, size):
            inside = [jnp.where((s >= low) & (s < low + size), 1, 0) for s in start]
            return jnp.where(sum(inside) == 0, 1.0, 0.0).astype(F32)

        chip_base = (me // 2) * (2 * tok)
        span = 4 * tok
        ring_base = ring * span
        keep_core0 = keep(chip_base, tok)
        keep_core1 = keep(chip_base + tok, tok)
        keep_chip0 = keep(ring_base, 2 * tok)
        keep_chip1 = keep(ring_base + 2 * tok, 2 * tok)
        keep_ring = keep(ring_base, span)
        keep_local = keep(MID * span, ring_base - MID * span)
        one, nil = jnp.float32(1.0), jnp.float32(0.0)
        keep_rear = jnp.where(ring >= MID, nil, keep(ring_base + span, (MID - 1 - ring) * span))
        first_core, first_half = core == 0, half == 0
        a_own = jnp.where(first_core, keep_core1, one)
        a_in = jnp.where(first_core, one, keep_core1)
        b_own = jnp.where(first_half, keep_chip1, one)
        b_in = jnp.where(first_half, one, keep_chip1)
        e_own, e_scan = jnp.where(first_half, one, nil), jnp.where(first_half, keep_chip0, one)
        p_in, p_scan = jnp.where(first_half, nil, one), jnp.where(first_half, one, keep_chip0)
        f_own, f_pre = jnp.where(first_core, one, nil), jnp.where(first_core, keep_core0, one)
        g_in, g_pre = jnp.where(first_core, nil, one), jnp.where(first_core, one, keep_core0)

        def segment(pos):
            return sum((s <= pos).astype(jnp.int32) for s in start)

        row = lax.broadcasted_iota(jnp.int32, (tok, 1), 0) + base
        col = lax.broadcasted_iota(jnp.int32, (1, tok), 1) + base
        seg_row, seg_col = segment(row), segment(col)
        prior = sum(jnp.where(s < base, 1, 0) for s in start)
        last = sum(jnp.where(s < base + tok, 1, 0) for s in start)
        use = jnp.where(seg_row == prior, 1.0, 0.0).astype(F32)
        allowed = (row >= col) & (seg_row == seg_col)
        keep_rows = jnp.where(seg_row == last, 1.0, 0.0).astype(k_ref.dtype)

        def send_core(j):
            z = 1 - half
            return remote(own.at[head_rows(group(1 - core, z) + j)], core_in.at[head_rows(z * OWN + j)],
                          core_sent, core_got.at[j], twin)

        def send_rest():
            return remote(own.at[group_rows(1 - core, half)], core_in.at[pl.ds(half * OWN * HD, OWN * HD)],
                          core_sent, core_got.at[OWN], twin)

        def send_chip(i):
            return remote(chip_far.at[rows_at(i)], chip_in.at[rows_at(i)],
                          chip_sent, chip_got.at[i], across)

        def send_fore(i):
            return remote(fore_out.at[rows_at(i)], fore_in.at[rows_at(i)],
                          fore_sent, ring_got.at[i], ahead)

        def local_lane(place):
            return jnp.where(place == last_fore, CHUNKS, 0)

        def send_local(i, place):
            return remote(local_out.at[rows_at(i)], local_in.at[rows_at(i)],
                          local_sent, ring_got.at[local_lane(place) + i], ahead)

        def send_rear(i):
            return remote(rear_out.at[rows_at(i)], rear_in.at[rows_at(i)],
                          rear_sent, ring_got.at[CHUNKS + i], behind)

        def send_back(i):
            return remote(back_out.at[rows_at(i)], back_in.at[rows_at(i)],
                          back_sent, back_got.at[i], across)

        def send_carry(n):
            return remote(core_out.at[head_rows(n)], carry_in.at[head_rows(n)],
                          carry_sent, carry_got.at[n], twin)

        def summaries(n):
            fetch_keys[n].wait()
            fetch_values[n].wait()
            first = group(*order[n])
            states = []
            for j in range(OWN):
                cols = head_cols(first + j)
                states.append(lax.dot_general(
                    k_ref[:, cols] * keep_rows, v_ref[:, cols],
                    (((0,), (0,)), ((), ())), preferred_element_type=F32))
            for j in range(OWN):
                own[head_rows(first + j)] = states[j]

        if first:
            summaries(0)
            greeted = jnp.where(ring < RING - 1, 1, 0) + jnp.where(rear_lands((ring + RING - 1) % RING), 1, 0)
            pl.semaphore_wait(barrier, 2 + greeted)
            for j in range(OWN):
                send_core(j).start()
            summaries(1)

        def chip_total(z, j):
            return a_own * own[head_rows(group(core, z) + j)] + a_in * core_in[head_rows(z * OWN + j)]

        def far(j, _):
            send_core(j).wait_recv()
            chip_far[head_rows(j)] = chip_total(1 - half, j)
            for s in range(SUB):
                send_chip(j * SUB + s).start()
            return 0

        def near(j, _):
            chip_own[head_rows(j)] = chip_total(half, j)
            return 0

        if first:
            lax.fori_loop(0, OWN, far, 0)
            summaries(2)
            send_rest().start()
            summaries(3)

            @pl.when(ring == 0)
            def _():
                fore_in[...] = jnp.zeros_like(fore_in)

            @pl.when(ring == MID)
            def _():
                local_in[...] = jnp.zeros_like(local_in)

            @pl.when(ring == MID - 1)
            def _():
                rear_in[...] = jnp.zeros_like(rear_in)

        def intra(n, _):
            cols = [head_cols(n * 8 + m) for m in range(8)]
            scores = [lax.dot_general(
                q_ref[:, c], k_ref[:, c], (((1,), (1,)), ((), ())), preferred_element_type=F32)
                for c in cols]
            weights = [jnp.where(allowed, s, 0.0).astype(v_ref.dtype) for s in scores]
            values = [jnp.dot(w, v_ref[:, c], preferred_element_type=F32) for w, c in zip(weights, cols)]
            for c, value in zip(cols, values):
                mixed[:, c] = value
            return 0

        if first:
            for fetch in fetch_rest:
                fetch.wait()
            squares[...] = jnp.zeros_like(squares)
            lax.fori_loop(0, HEADS // 8, intra, 0)
            send_rest().wait_recv()
            lax.fori_loop(0, OWN, near, 0)

        def spread(z, i, prefix):
            n = z * CHUNKS + i
            core_out[rows_at(n)] = f_own * own[rows_at(group(core, z) * SUB + i)] + f_pre * prefix
            carry[rows_at(n)] = (g_in * core_in[rows_at(n)] + g_pre * prefix).astype(carry.dtype)

            @pl.when(i % SUB == SUB - 1)
            def _():
                send_carry(z * OWN + i // SUB).start()

        def finish(i, prefix):
            arrived, mine = chip_in[rows_at(i)], chip_own[rows_at(i)]
            back_out[rows_at(i)] = e_own * mine + e_scan * prefix
            send_back(i).start()
            spread(half, i, p_in * arrived + p_scan * prefix)

        lag_local = HOP * (ring - MID)
        late = jnp.where(lax.axis_index("sess") == 0, LATE, 0)
        lag_fore = HOP * ring + jnp.where(ring == 0, 0, late)
        lag_rear = HOP * ((RING + MID - 1 - ring) % RING) - jnp.where(ring == 0, late, 0)
        ends = (ring > MID) & (ring < RING - 1)
        lag_prefix = jnp.where(ring <= last_fore, lag_fore, lag_rear)
        lag_back = jnp.where(ends, lag_prefix + BACK, jnp.maximum(lag_prefix + 2 * BACK, DRAINED))
        lag_join = lag_back + SUB + JOIN

        def settle(j):
            heads, states = [], []
            for z in (half, 1 - half):
                heads.append(group(core, z) + j)
                states.append(carry[head_rows(z * OWN + j)])
            for z in (half, 1 - half):
                send_carry(z * OWN + j).wait_recv()
                heads.append(group(1 - core, z) + j)
                states.append(carry_in[head_rows(z * OWN + j)].astype(carry.dtype))
            cols = [head_cols(h) for h in heads]
            inter = [jnp.dot(q_ref[:, c], state, preferred_element_type=F32) for c, state in zip(cols, states)]
            values = [mixed[:, c] + use * part for c, part in zip(cols, inter)]
            for c, value in zip(cols, values):
                mixed[:, c] = value
            squares[...] += sum(value * value for value in values)

        def active(s, lag):
            return (s >= lag) & (s < lag + CHUNKS)

        def step(s, _):
            if first:
                @pl.when(s < CHUNKS)
                def _():
                    send_chip(s).wait_recv()
                    total[rows_at(s)] = b_own * chip_own[rows_at(s)] + b_in * chip_in[rows_at(s)]

                @pl.when((ring >= MID) & active(s, lag_local))
                def _():
                    i = s - lag_local

                    @pl.when(ring > MID)
                    def _():
                        send_local(i, ring).wait_recv()

                    @pl.when(ring < RING - 1)
                    def _():
                        local_out[rows_at(i)] = total[rows_at(i)] + keep_ring * local_in[rows_at(i)]
                        send_local(i, ring + 1).start()

                @pl.when((ring <= last_fore) & active(s, lag_fore))
                def _():
                    i = s - lag_fore

                    @pl.when(ring > 0)
                    def _():
                        send_fore(i).wait_recv()

                    prefix = fore_in[rows_at(i)]

                    @pl.when(ring < last_fore)
                    def _():
                        fore_out[rows_at(i)] = total[rows_at(i)] + keep_ring * prefix
                        send_fore(i).start()

                    finish(i, prefix)

                @pl.when(((ring < MID) | (ring > last_fore)) & active(s, lag_rear))
                def _():
                    i = s - lag_rear

                    @pl.when(ring != MID - 1)
                    def _():
                        send_rear(i).wait_recv()

                    @pl.when((ring < MID) | (ring == RING - 1))
                    def _():
                        rear_out[rows_at(i)] = rear_in[rows_at(i)] + keep_rear * total[rows_at(i)]
                        send_rear(i).start()

                    @pl.when(ring > last_fore)
                    def _():
                        finish(i, local_in[rows_at(i)] + keep_local * rear_in[rows_at(i)])

            @pl.when(active(s, lag_back))
            def _():
                i = s - lag_back
                send_back(i).wait_recv()
                spread(1 - half, i, back_in[rows_at(i)])

            @pl.when((s >= lag_join) & ((s - lag_join) % SUB == 0))
            def _():
                settle((s - lag_join) // SUB)

            return 0

        streamed = CHUNKS + jnp.maximum(
            jnp.where(ring <= last_fore, lag_fore, 0),
            jnp.where((ring < MID) | (ring > last_fore), lag_rear, 0))
        if first:
            lax.fori_loop(0, streamed, step, 0)
        else:
            lax.fori_loop(streamed, lag_join + CHUNKS - SUB + 1, step, 0)

    pl.run_scoped(
        lambda *got: phase(True, *got),
        pltpu.SemaphoreType.DMA((OWN + 1,)), pltpu.SemaphoreType.DMA((CHUNKS,)), pltpu.SemaphoreType.DMA((2 * CHUNKS,)))
    phase(False)
    mean = jnp.sum(squares[...], axis=-1, keepdims=True) * (1.0 / (HEADS * HD))
    scale = lax.rsqrt(mean + 1e-05)
    for h in range(HEADS):
        cols = slice(h * HD, (h + 1) * HD)
        out_ref[:, cols] = (mixed[:, cols] * scale * gain_ref[:, cols]).astype(out_ref.dtype)

    for z in range(2):
        remote(own.at[group_rows(1 - core, z)], core_in.at[pl.ds(z * OWN * HD, OWN * HD)],
               core_sent, back_got.at[0], twin).wait_send()
    remote(chip_far, chip_in, chip_sent, back_got.at[0], across).wait_send()
    remote(back_out, back_in, back_sent, back_got.at[0], across).wait_send()
    remote(core_out, carry_in, carry_sent, carry_got.at[0], twin).wait_send()

    @pl.when(ring < last_fore)
    def _():
        remote(fore_out, fore_in, fore_sent, back_got.at[0], ahead).wait_send()

    @pl.when((ring >= MID) & (ring < RING - 1))
    def _():
        remote(local_out, local_in, local_sent, back_got.at[0], ahead).wait_send()

    @pl.when((ring < MID) | (ring == RING - 1))
    def _():
        remote(rear_out, rear_in, rear_sent, back_got.at[0], behind).wait_send()


def shards(query_rows, key_rows, value_rows, seg_starts, norm_gain):
    _, tok, width = query_rows.shape
    dma = pltpu.SemaphoreType.DMA
    hbm = pl.BlockSpec(memory_space=pltpu.HBM)
    block = pltpu.VMEM((tok, width), key_rows.dtype)
    states = lambda heads: pltpu.VMEM((heads * HD, HD), F32)
    one = dma(())
    stay = lambda x: pltpu.with_memory_space_constraint(x, pltpu.HBM)
    out = pl.pallas_call(
        kernel,
        out_shape=jax.ShapeDtypeStruct((tok, width), query_rows.dtype),
        in_specs=[hbm] * 5,
        out_specs=pl.BlockSpec(memory_space=pltpu.VMEM),
        scratch_shapes=[
            pltpu.SMEM((1, 4), jnp.int32), block, block, block, pltpu.VMEM((1, width), F32),
            states(HEADS), states(2 * OWN),
            states(OWN), states(OWN), states(OWN), states(OWN),
            states(OWN), states(OWN), states(OWN), states(OWN), states(OWN), states(OWN),
            states(OWN), states(OWN), states(2 * OWN), states(2 * OWN),
            pltpu.VMEM((2 * OWN * HD, HD), jnp.bfloat16),
            pltpu.VMEM((tok, width), F32), pltpu.VMEM((tok, HD), F32),
            dma((11,)),
            one, one, one, one, one, one, dma((CHUNKS,)), one, dma((2 * OWN,)),
        ],
        compiler_params=pltpu.CompilerParams(
            collective_id=0, has_side_effects=True, vmem_limit_bytes=32 * 1024 * 1024),
    )(stay(seg_starts), stay(query_rows[0]), stay(key_rows[0]), stay(value_rows[0]),
      stay(norm_gain.reshape(1, width)))
    return out.reshape(1, tok, width)


def solution(mesh):
    placed = (
        P("sess", "ctx", None),
        P("sess", "ctx", None),
        P("sess", "ctx", None),
        P("sess", None),
        P(),
    )
    return jax.shard_map(
        shards, mesh=mesh, in_specs=placed, out_specs=P("sess", "ctx", None), check_vma=False
    )
```
